512 devices in a mesh: rows: 64 (over y, z_lo, core), feat: 8 (over x, z_hi).
Axes of the slice: x: 4, y: 4, z: 16 (z_hi: 2, z_lo: 8; z = z_hi * 8 + z_lo), core: 2. Of those that a mesh axis runs over, the one named last changes fastest.
Arguments:
- logits: float32 [196608, 32], P('rows'), may hold values from -6 to 6
- labels: int32 [196608], P('rows'), may hold values from 0 to 31
- node_ids: int32 [196608], P('rows'), may hold values from 0 to 7
- bin_codes: int32 [196608, 256], P('rows', 'feat'), may hold values from 0 to 63
- split_feature: int32 [8], replicated, may hold values from 0 to 255
- split_bin: int32 [8], replicated, may hold values from 1 to 63
- split_missing: int32 [8], replicated, may hold values from 0 to 1
Outputs:
- new_logits: float32 [196608, 32], P('rows')
- gain_table: float32 [64, 32, 128], P('rows', 'feat')
- leaves: float32 [8, 2, 32], replicated
The draws below stay inside these ranges and needn't reach their ends.
Inputs may be any that keep to these rules, and one draw needn't show every extreme that they name: `split_missing`: 1 sends the missing code 64 - 1 to the left child, 0 to the right child.
All inputs are finite; a program needn't handle non-finite values.
Results may differ from the reference program's by a relative error of at most 0.0014.
Values sent between devices are 32-bit elements; how exact they have to be, the bound alone decides.
A program may use at most 64 MiB of HBM per device.

```python
import math
import jax
import jax.numpy as jnp
import numpy as np
from jax import lax

K = 32
FEAT = 256
BINS = 64
NODES = 8
TOTAL_ROWS = 196608
N_ROWS = 64
N_FEAT = 8


def place_ends(array, key, smallest, largest):
    dims = array.shape
    place = [jax.random.randint(jax.random.fold_in(key, axis), (), 0, dims[axis]) for axis in range(len(dims))]
    array = array.at[tuple(place)].set(smallest)
    longest = dims.index(max(dims))
    place[longest] = (place[longest] + 1) % dims[longest]
    return array.at[tuple(place)].set(largest)


def levels(key, extent, cuts, low, high):
    def one(dim, parts):
        draws = jax.random.uniform(jax.random.fold_in(jax.random.fold_in(key, 6), dim), (parts,), jnp.float32, low / len(cuts), high / len(cuts))
        return jnp.repeat(jnp.exp(draws), extent[dim] // parts).reshape((-1,) + (1,) * (len(extent) - dim - 1))

    level = one(*cuts[0])
    for cut in cuts[1:]:
        level = level * one(*cut)
    return level


def rank_bounds(amount, slope):
    loads = [(1 << 20) // math.isqrt(rank ** slope) + 1 for rank in range(1, amount + 1)]
    scale = 1 + sum(loads) // (1 << 30)
    return np.cumsum(np.array([max(1, weight // scale) for weight in loads]))


def ranked_ids(stream_key, shape, number_of, slope):
    table = rank_bounds(number_of, slope)
    lot = jax.random.randint(jax.random.fold_in(stream_key, 1), shape, 0, int(table[number_of - 1]))
    standing = jnp.searchsorted(jnp.asarray(table, jnp.int32), lot, side="right")
    return jax.random.permutation(jax.random.fold_in(stream_key, 2), number_of)[standing].astype(jnp.int32)


def gaussian(stream_key, shape, width, most, split=(), kind=jnp.bfloat16):
    entries = jax.random.normal(stream_key, shape, jnp.float32) * width
    if len(split) > 0:
        entries = levels(stream_key, shape, split, -0.22, 0.18) * entries
    return jnp.clip(entries, min=-most, max=most).astype(kind)


def setup_inputs(seed: int = 0) -> dict:
    key_of = jax.random.split(jax.random.key(seed), 8)
    return {
        "logits": gaussian(key_of[0], (TOTAL_ROWS, K), 1.5, 6.0, ((0, 64),), jnp.float32),
        "labels": place_ends(ranked_ids(key_of[1], (TOTAL_ROWS,), K, 2), jax.random.fold_in(key_of[1], 3), 0, K - 1).astype(jnp.int32),
        "node_ids": place_ends(ranked_ids(key_of[2], (TOTAL_ROWS,), NODES, 1), jax.random.fold_in(key_of[2], 3), 0, NODES - 1).astype(jnp.int32),
        "bin_codes": place_ends(ranked_ids(key_of[3], (TOTAL_ROWS, FEAT), BINS, 2), jax.random.fold_in(key_of[3], 3), 0, BINS - 1).astype(jnp.int32),
        "split_feature": place_ends(jax.random.randint(key_of[4], (NODES,), 0, FEAT), jax.random.fold_in(key_of[4], 1), 0, FEAT - 1).astype(jnp.int32),
        "split_bin": place_ends(jax.random.randint(key_of[5], (NODES,), 1, BINS), jax.random.fold_in(key_of[5], 1), 1, BINS - 1).astype(jnp.int32),
        "split_missing": place_ends(jax.random.randint(key_of[6], (NODES,), 0, 2), jax.random.fold_in(key_of[6], 1), 0, 1).astype(jnp.int32),
    }


reg_lambda = 1.0
step_size = 0.3


def gradients(logits, labels):
    expo_vals = jnp.exp(logits)
    soft_prob = expo_vals / jnp.sum(expo_vals, axis=1, keepdims=True)
    target = (labels[:, None] == jnp.arange(K, dtype=jnp.int32)[None, :]).astype(jnp.float32)
    grad_rows = (soft_prob - target).astype(jnp.bfloat16)
    hess_rows = (soft_prob * (1.0 - soft_prob)).astype(jnp.bfloat16)
    return jnp.concatenate([grad_rows, hess_rows], axis=1)


def split_score(sums):
    grad_part = sums[..., :K]
    hess_part = sums[..., K:]
    return jnp.sum(grad_part * grad_part / (hess_part + reg_lambda), axis=-1)


def reference(logits, labels, node_ids, bin_codes, split_feature, split_bin, split_missing):
    grad_hess = gradients(logits, labels).astype(jnp.float32)

    def feature_hist(codes):
        return jax.ops.segment_sum(grad_hess, node_ids * BINS + codes, num_segments=NODES * BINS)

    hist = lax.map(feature_hist, bin_codes.T)
    hist = hist.reshape(FEAT, NODES, BINS, 2 * K).transpose(1, 0, 2, 3)
    cumul = jnp.cumsum(hist[:, :, :BINS - 1, :], axis=2)
    left_base = jnp.concatenate([jnp.zeros_like(hist[:, :, :1, :]), cumul], axis=2)
    node_total = jnp.sum(hist, axis=2, keepdims=True)
    missing_sum = hist[:, :, BINS - 1:, :]
    left_miss = left_base + missing_sum
    parent_score = split_score(node_total)
    gain_left = split_score(left_miss) + split_score(node_total - left_miss) - parent_score
    gain_right = split_score(left_base) + split_score(node_total - left_base) - parent_score
    gain = jnp.concatenate([gain_left, gain_right], axis=-1) / (2.0 * K)
    per_node = N_ROWS // NODES
    pairs_dev = FEAT // N_FEAT // per_node
    gain = gain.reshape(NODES, N_FEAT, per_node, pairs_dev, 2 * BINS).transpose(0, 2, 1, 3, 4)
    gain_table = gain.reshape(N_ROWS, N_FEAT * pairs_dev, 2 * BINS)

    chosen = hist[jnp.arange(NODES, dtype=jnp.int32), split_feature]
    bin_iota = jnp.arange(BINS, dtype=jnp.int32)
    bin_mask = ((bin_iota[None, :] < split_bin[:, None]) & (bin_iota[None, :] < BINS - 1)).astype(jnp.float32)
    left_sum = jnp.sum(chosen * bin_mask[:, :, None], axis=1) + chosen[:, BINS - 1, :] * split_missing[:, None].astype(jnp.float32)
    node_sum = jnp.sum(chosen, axis=1)
    side_sums = jnp.stack([left_sum, node_sum - left_sum], axis=1)
    leaves = -side_sums[..., :K] / (side_sums[..., K:] + reg_lambda)

    row_feature = split_feature[node_ids]
    row_code = jnp.take_along_axis(bin_codes, row_feature[:, None], axis=1)[:, 0]
    goes_left = (row_code < split_bin[node_ids]) | ((row_code == BINS - 1) & (split_missing[node_ids] == 1))
    row_side = jnp.where(goes_left, 0, 1).astype(jnp.int32)
    new_logits = logits + step_size * leaves[node_ids, row_side]
    return (new_logits, gain_table, leaves)
```

```python
import jax
import jax.numpy as jnp
from jax import lax
from jax.experimental import pallas as pl
from jax.experimental.pallas import tpu as pltpu
from jax.sharding import PartitionSpec as P

BINS = 64
MESH = pl.DeviceIdType.MESH
reg_lambda = 1.0
step_size = 0.3
LANE_BLOCK = 512
NT = (((1,), (1,)), ((), ()))
NN = (((1,), (0,)), ((), ()))


def split3(x):
    hi = x.astype(jnp.bfloat16)
    rest = x - hi.astype(jnp.float32)
    mid = rest.astype(jnp.bfloat16)
    low = (rest - mid.astype(jnp.float32)).astype(jnp.bfloat16)
    return hi, mid, low


def exact_dot(x, weights, dims):
    hi, mid, low = split3(x)
    dot = lambda part: lax.dot_general(part, weights, dims, preferred_element_type=jnp.float32)
    return dot(hi) + (dot(mid) + dot(low))


def ratio(sums):
    grad_part = sums[:32]
    hess_part = sums[32:]
    return jnp.sum(grad_part * grad_part / (hess_part + reg_lambda), axis=0, keepdims=True)


def kernel(
    feature_ref,
    bin_ref,
    missing_ref,
    logits_ref,
    labels_ref,
    nodes_ref,
    codes_ref,
    new_ref,
    gain_ref,
    leaves_ref,
    masked,
    hot,
    hist,
    core_buf,
    y1_buf,
    y2_buf,
    z1_buf,
    z2_buf,
    z3_buf,
    flag_buf,
    s1_buf,
    s2_buf,
    s3_buf,
    core_send,
    core_recv,
    y1_send,
    y1_recv,
    y2_send,
    y2_recv,
    z1_send,
    z1_recv,
    z2_send,
    z2_recv,
    z3_send,
    z3_recv,
    flag_send,
    flag_recv,
    s1_send,
    s1_recv,
    s2_send,
    s2_recv,
    s3_send,
    s3_recv,
):
    rows = logits_ref.shape[1]
    row = lax.axis_index("rows")
    feat = lax.axis_index("feat")
    core = row % 2
    z = (row // 2) % 8
    y = row // 16
    z0, z1, z2 = z % 2, (z // 2) % 2, z // 4
    group = y * 2 + core
    ya = y + 1 - 2 * (y % 2)
    yb = 3 - y
    yc = 3 - ya

    def at_y(other):
        return other * 16 + z * 2 + core

    core_peer = row + 1 - 2 * core
    z_peer1 = row + 2 * (1 - 2 * z0)
    z_peer2 = row + 4 * (1 - 2 * z1)
    z_peer4 = row + 8 * (1 - 2 * z2)

    def feat_peer(d):
        return (row, (feat + d) % 8)

    def group_peer(d):
        other = (group + d) % 8
        return ((other // 2) * 16 + z * 2 + other % 2, feat)

    def z_peer(d):
        return (y * 16 + ((z + d) % 8) * 2 + core, feat)

    barrier = pltpu.get_barrier_semaphore()
    for d in range(1, 8):
        for peer in (feat_peer(d), group_peer(d), z_peer(d)):
            pl.semaphore_signal(barrier, inc=1, device_id=peer, device_id_type=MESH)

    iota16 = lax.broadcasted_iota(jnp.int32, (16, LANE_BLOCK), 0)
    iota32 = lax.broadcasted_iota(jnp.int32, (32, LANE_BLOCK), 0)
    one, zero = jnp.float32(1.0), jnp.float32(0.0)

    def prepare(i, side_sums):
        at = pl.ds(pl.multiple_of(i * LANE_BLOCK, LANE_BLOCK), LANE_BLOCK)
        expo = jnp.exp(logits_ref[:, at])
        prob = expo / jnp.sum(expo, axis=0, keepdims=True)
        target = jnp.where(iota32 == labels_ref[:, at], one, zero)
        grad = (prob - target).astype(jnp.bfloat16).astype(jnp.float32)
        hess = (prob * (1.0 - prob)).astype(jnp.bfloat16).astype(jnp.float32)
        both = jnp.concatenate([grad, hess], axis=0)
        node = nodes_ref[:, at]
        row_feature = jnp.zeros_like(node)
        row_bin = jnp.zeros_like(node)
        row_missing = jnp.zeros_like(node)
        for n in range(8):
            here = node == n
            masked[n * 64 : (n + 1) * 64, at] = jnp.where(here, both, zero).astype(jnp.bfloat16)
            row_feature = jnp.where(here, feature_ref[n], row_feature)
            row_bin = jnp.where(here, bin_ref[n], row_bin)
            row_missing = jnp.where(here, missing_ref[n], row_missing)
        column = row_feature - feat * 32
        owned = (column >= 0) & (column < 32)
        code = jnp.sum(
            jnp.where(iota32 == column, codes_ref[:, at].astype(jnp.float32), zero),
            axis=0,
            keepdims=True,
        ).astype(jnp.int32)
        left = (code < row_bin) | ((code == BINS - 1) & (row_missing == 1))
        right = jnp.where(left, 0, 1)
        flag_buf[feat, :, at] = jnp.where(owned, right, 0).astype(jnp.float32)
        slot = jnp.where(owned, node * 2 + right, -1)
        slot_hot = jnp.where(iota16 == slot, one, zero).astype(jnp.bfloat16)
        return side_sums + lax.dot_general(
            slot_hot, both.astype(jnp.bfloat16), NT, preferred_element_type=jnp.float32
        )

    side_sums = lax.fori_loop(
        0, rows // LANE_BLOCK, prepare, jnp.zeros((16, 64), jnp.float32)
    )
    s1_buf[feat] = jnp.concatenate([side_sums, jnp.zeros((16, 64), jnp.float32)], axis=1)

    pl.semaphore_wait(barrier, 21)

    def exchange(buf, send, recv, mine, peer):
        def copy(d, slot):
            return pltpu.make_async_remote_copy(
                src_ref=buf.at[slot],
                dst_ref=buf.at[slot],
                send_sem=send.at[d - 1],
                recv_sem=recv.at[slot],
                device_id=peer(d),
                device_id_type=MESH,
            )

        def start():
            for d in range(1, 8):
                copy(d, mine).start()

        def arrive():
            for d in range(1, 8):
                copy(d, (mine + d) % 8).wait_recv()

        def finish():
            for d in range(1, 8):
                copy(d, mine).wait_send()

        return start, arrive, finish

    flags = exchange(flag_buf, flag_send, flag_recv, feat, feat_peer)
    stage1 = exchange(s1_buf, s1_send, s1_recv, feat, feat_peer)
    stage2 = exchange(s2_buf, s2_send, s2_recv, group, group_peer)
    stage3 = exchange(s3_buf, s3_send, s3_recv, z, z_peer)
    stage1[0]()
    flags[0]()

    def total(buf):
        sums = buf[0]
        for i in range(1, 8):
            sums = sums + buf[i]
        return sums

    def remote(src, dst, send, recv, peer):
        return pltpu.make_async_remote_copy(
            src_ref=src,
            dst_ref=dst,
            send_sem=send,
            recv_sem=recv,
            device_id=(peer, feat),
            device_id_type=MESH,
        )

    def core_copy(k):
        return remote(
            hist.at[2 * k], core_buf.at[k], core_send.at[k], core_recv.at[k], core_peer
        )

    def first_y(k):
        colour = k % 2
        return ya + colour * (yb - ya)

    def second_y(k):
        colour = k % 2
        return yb + colour * (ya - yb)

    def y1_copy(k, part):
        dest = first_y(k) if part else yc
        return remote(
            hist.at[2 * k + 1, :, pl.ds(2 * dest, 2)],
            y1_buf.at[k, part],
            y1_send.at[k, part],
            y1_recv.at[k, part],
            at_y(first_y(k)),
        )

    def y2_copy(k):
        dest = second_y(k)
        return remote(
            hist.at[2 * k + 1, :, pl.ds(2 * dest, 2)],
            y2_buf.at[k],
            y2_send.at[k],
            y2_recv.at[k],
            at_y(dest),
        )

    mine_y = pl.ds(2 * y, 2)

    def z1_copy(colour):
        k = 2 * (1 - z0) + colour
        return remote(
            hist.at[2 * k + 1, :, mine_y],
            z1_buf.at[colour],
            z1_send.at[colour],
            z1_recv.at[colour],
            z_peer1,
        )

    def z2_copy(colour):
        k = 2 * z0 + colour
        return remote(
            hist.at[2 * k + 1, 1 - z1, mine_y],
            z2_buf.at[colour],
            z2_send.at[colour],
            z2_recv.at[colour],
            z_peer2,
        )

    def z3_copy(colour):
        k = 2 * z0 + colour
        return remote(
            hist.at[2 * k + 1, z1, 2 * y + 1 - z2],
            z3_buf.at[colour],
            z3_send.at[colour],
            z3_recv.at[colour],
            z_peer4,
        )

    iota64 = lax.broadcasted_iota(jnp.int32, (64, rows), 0)

    def after_core(k):
        core_copy(k).wait_recv()
        hist[2 * k + 1] = hist[2 * k + 1] + core_buf[k]
        y1_copy(k, 0).start()
        y1_copy(k, 1).start()

    def step(s, carry):
        k = s // 2
        side = s % 2
        half, colour = k // 2, k % 2
        owner = side * core + (1 - side) * (1 - core)
        base = half * 8 + owner * 4 + colour * 2
        for high in range(2):
            for low in range(2):
                code = codes_ref[pl.ds(base + 16 * high + low, 1), :]
                start = (high * 2 + low) * 64
                hot[start : start + 64, :] = jnp.where(code == iota64, one, zero).astype(
                    jnp.bfloat16
                )
        out = lax.dot_general(masked[...], hot[...], NT, preferred_element_type=jnp.float32)
        for high in range(2):
            for n in range(8):
                hist[s, high, n] = out[n * 64 : (n + 1) * 64, high * 128 : (high + 1) * 128]

        @pl.when(side == 0)
        def _():
            core_copy(k).start()

        @pl.when((side == 0) & (k > 0))
        def _():
            after_core(k - 1)

        return carry

    lax.fori_loop(0, 8, step, 0)
    after_core(3)

    def after_y1(k):
        y1_copy(k, 0).wait_recv()
        at = pl.ds(2 * second_y(k), 2)
        hist[2 * k + 1, :, at] = hist[2 * k + 1, :, at] + y1_buf[k, 0]
        y2_copy(k).start()
        y1_copy(k, 1).wait_recv()
        hist[2 * k + 1, :, mine_y] = hist[2 * k + 1, :, mine_y] + y1_buf[k, 1]

    def after_y2(k):
        y2_copy(k).wait_recv()
        hist[2 * k + 1, :, mine_y] = hist[2 * k + 1, :, mine_y] + y2_buf[k]

        @pl.when(z0 != k // 2)
        def _():
            z1_copy(k % 2).start()

    def after_z1(colour):
        z1_copy(colour).wait_recv()
        k = 2 * z0 + colour
        hist[2 * k + 1, :, mine_y] = hist[2 * k + 1, :, mine_y] + z1_buf[colour]
        z2_copy(colour).start()

    def after_z2(colour):
        z2_copy(colour).wait_recv()
        k = 2 * z0 + colour
        hist[2 * k + 1, z1, mine_y] = hist[2 * k + 1, z1, mine_y] + z2_buf[colour]
        z3_copy(colour).start()

    stage1[1]()
    s2_buf[group] = total(s1_buf)
    stage2[0]()
    after_y1(0)
    after_y1(1)
    stage2[1]()
    s3_buf[z] = total(s2_buf)
    stage3[0]()
    after_y2(0)
    after_y2(1)
    after_y1(2)
    after_y1(3)

    stage3[1]()
    flags[1]()
    sums = total(s3_buf)
    sums_t = jnp.transpose(sums)[:64, :]
    leaves_t = -sums_t[:32] / (sums_t[32:] + reg_lambda)
    leaves = jnp.transpose(leaves_t)
    for n in range(8):
        leaves_ref[n] = leaves[2 * n : 2 * n + 2, :]

    def update(i, carry):
        at = pl.ds(pl.multiple_of(i * LANE_BLOCK, LANE_BLOCK), LANE_BLOCK)
        count = flag_buf[0, :, at]
        for j in range(1, 8):
            count = count + flag_buf[j, :, at]
        slot = nodes_ref[:, at] * 2 + jnp.where(count > 0.5, 1, 0)
        slot_hot = jnp.where(iota16 == slot, one, zero).astype(jnp.bfloat16)
        new_ref[:, at] = logits_ref[:, at] + step_size * exact_dot(leaves_t, slot_hot, NN)
        return carry

    lax.fori_loop(0, rows // LANE_BLOCK, update, 0)

    after_y2(2)
    after_y2(3)
    after_z1(0)
    after_z1(1)
    after_z2(0)
    after_z2(1)

    lane_in = lax.broadcasted_iota(jnp.int32, (128, 128), 0)
    lane_out = lax.broadcasted_iota(jnp.int32, (128, 128), 1)
    same = (lane_in // BINS) == (lane_out // BINS)
    bin_in, bin_out = lane_in % BINS, lane_out % BINS
    as_weights = lambda mask: jnp.where(mask, one, zero).astype(jnp.bfloat16)
    lower = as_weights(same & (bin_in < bin_out) & (bin_in < BINS - 1))
    every = as_weights(same)
    last = as_weights(same & (bin_in == BINS - 1))
    lane = lax.broadcasted_iota(jnp.int32, (1, 128), 1)
    for colour in range(2):
        z3_copy(colour).wait_recv()
        k = 2 * z0 + colour
        owned = hist[2 * k + 1, z1, 2 * y + z2] + z3_buf[colour]
        left_base = exact_dot(owned, lower, NN)
        node_total = exact_dot(owned, every, NN)
        left_miss = left_base + exact_dot(owned, last, NN)
        parent = ratio(node_total)
        gain_left = (ratio(left_miss) + ratio(node_total - left_miss) - parent) / 64.0
        gain_right = (ratio(left_base) + ratio(node_total - left_base) - parent) / 64.0
        gain_ref[0, 2 * colour : 2 * colour + 1, :] = jnp.where(
            lane < BINS, gain_left, pltpu.roll(gain_right, BINS, 1)
        )
        gain_ref[0, 2 * colour + 1 : 2 * colour + 2, :] = jnp.where(
            lane < BINS, pltpu.roll(gain_left, BINS, 1), gain_right
        )

    for stage in (flags, stage1, stage2, stage3):
        stage[2]()
    for k in range(4):
        core_copy(k).wait_send()
        y1_copy(k, 0).wait_send()
        y1_copy(k, 1).wait_send()
        y2_copy(k).wait_send()
    for colour in range(2):
        z1_copy(colour).wait_send()
        z2_copy(colour).wait_send()
        z3_copy(colour).wait_send()


def local(logits, labels, node_ids, bin_codes, split_feature, split_bin, split_missing):
    rows = logits.shape[0]
    f32 = jnp.float32
    vmem = pl.BlockSpec(memory_space=pltpu.VMEM)
    smem = pl.BlockSpec(memory_space=pltpu.SMEM)
    dma = pltpu.SemaphoreType.DMA
    new_t, gains, leaves = pl.pallas_call(
        kernel,
        out_shape=(
            jax.ShapeDtypeStruct((32, rows), f32),
            jax.ShapeDtypeStruct((1, 4, 128), f32),
            jax.ShapeDtypeStruct((8, 2, 32), f32),
        ),
        in_specs=[smem] * 3 + [vmem] * 4,
        out_specs=(vmem, vmem, vmem),
        scratch_shapes=[
            pltpu.VMEM((512, rows), jnp.bfloat16),
            pltpu.VMEM((256, rows), jnp.bfloat16),
            pltpu.VMEM((8, 2, 8, 64, 128), f32),
            pltpu.VMEM((4, 2, 8, 64, 128), f32),
            pltpu.VMEM((4, 2, 2, 2, 64, 128), f32),
            pltpu.VMEM((4, 2, 2, 64, 128), f32),
            pltpu.VMEM((2, 2, 2, 64, 128), f32),
            pltpu.VMEM((2, 2, 64, 128), f32),
            pltpu.VMEM((2, 64, 128), f32),
            pltpu.VMEM((8, 1, rows), f32),
            pltpu.VMEM((8, 16, 128), f32),
            pltpu.VMEM((8, 16, 128), f32),
            pltpu.VMEM((8, 16, 128), f32),
            dma((4,)),
            dma((4,)),
            dma((4, 2)),
            dma((4, 2)),
            dma((4,)),
            dma((4,)),
        ]
        + [dma((2,))] * 6
        + [dma((7,)), dma((8,))] * 4,
        compiler_params=pltpu.CompilerParams(
            collective_id=0, has_side_effects=True, vmem_limit_bytes=48 * 1024 * 1024
        ),
    )(
        split_feature,
        split_bin,
        split_missing,
        logits.T,
        labels.reshape(1, rows),
        node_ids.reshape(1, rows),
        bin_codes.T,
    )
    return new_t.T, gains, leaves


def solution(mesh):
    return jax.shard_map(
        local,
        mesh=mesh,
        in_specs=(P("rows", None), P("rows"), P("rows"), P("rows", "feat"), P(), P(), P()),
        out_specs=(P("rows", None), P("rows", "feat", None), P()),
        check_vma=False,
    )
```

```python
import jax
import jax.numpy as jnp
from jax import lax
from jax.experimental import pallas as pl
from jax.experimental.pallas import tpu as pltpu
from jax.sharding import PartitionSpec as P

BINS = 64
MESH = pl.DeviceIdType.MESH
reg_lambda = 1.0
step_size = 0.3
LANE_BLOCK = 512
NT = (((1,), (1,)), ((), ()))
NN = (((1,), (0,)), ((), ()))


def split3(x):
    hi = x.astype(jnp.bfloat16)
    rest = x - hi.astype(jnp.float32)
    mid = rest.astype(jnp.bfloat16)
    low = (rest - mid.astype(jnp.float32)).astype(jnp.bfloat16)
    return hi, mid, low


def exact_dot(x, weights, dims):
    hi, mid, low = split3(x)
    dot = lambda part: lax.dot_general(part, weights, dims, preferred_element_type=jnp.float32)
    return dot(hi) + (dot(mid) + dot(low))


def ratio(sums):
    grad_part = sums[:32]
    hess_part = sums[32:]
    return jnp.sum(grad_part * grad_part / (hess_part + reg_lambda), axis=0, keepdims=True)


def kernel(
    feature_hbm,
    bin_hbm,
    missing_hbm,
    logits_hbm,
    labels_hbm,
    nodes_hbm,
    codes_hbm,
    new_hbm,
    gain_hbm,
    leaves_hbm,
    new_ref,
    gain_ref,
    leaves_ref,
    feature_ref,
    bin_ref,
    missing_ref,
    logits_ref,
    labels_ref,
    nodes_ref,
    codes_ref,
    masked,
    hot,
    hist,
    core_buf,
    y1_buf,
    y2_buf,
    z1_buf,
    direct_buf,
    flag_buf,
    far_flag,
    x_buf,
    group_buf,
    pair_buf,
    load_sem,
    store_sem,
    core_send,
    core_recv,
    y1_send,
    y1_recv,
    y2_send,
    y2_recv,
    z1_send,
    z1_recv,
    direct_send,
    direct_recv,
    flag_send,
    flag_recv,
    far_send,
    far_recv,
    x_send,
    x_recv,
    group_send,
    group_recv,
    pair_send,
    pair_recv,
    vouch4,
    vouch2,
):
    rows = logits_ref.shape[1]
    row = lax.axis_index("rows")
    feat = lax.axis_index("feat")
    core = row % 2
    z = (row // 2) % 8
    y = row // 16
    x, z_hi = feat // 2, feat % 2
    z0, z1, z2 = z % 2, (z // 2) % 2, z // 4
    quad = z // 2
    group = y * 2 + core
    ya = y + 1 - 2 * (y % 2)
    yb = 3 - y
    yc = 3 - ya

    loads = [
        pltpu.make_async_copy(src, dst, load_sem.at[i])
        for i, (src, dst) in enumerate(
            (
                (logits_hbm, logits_ref),
                (labels_hbm, labels_ref),
                (nodes_hbm, nodes_ref),
                (codes_hbm, codes_ref),
                (feature_hbm, feature_ref),
                (bin_hbm, bin_ref),
                (missing_hbm, missing_ref),
            )
        )
    ]
    for load in loads:
        load.start()
    stores = [
        pltpu.make_async_copy(src, dst, store_sem.at[i])
        for i, (src, dst) in enumerate(
            ((new_ref, new_hbm), (leaves_ref, leaves_hbm), (gain_ref, gain_hbm))
        )
    ]

    def at_y(other):
        return (other * 16 + z * 2 + core, feat)

    def at_z(other):
        return (y * 16 + other * 2 + core, feat)

    core_peer = (row + 1 - 2 * core, feat)
    z_peer1 = at_z(z + 1 - 2 * z0)
    z_peer2 = at_z(z + 2 - 4 * z1)
    z_peer4 = at_z(z + 4 - 8 * z2)
    far_peer = (row, x * 2 + 1 - z_hi)
    ring4 = (y * 16 + ((z + 4) % 8) * 2 + core, x * 2 + 1 - z_hi)

    def x_peer(d):
        return (row, ((x + d) % 4) * 2 + z_hi)

    def group_peer(d):
        other = (group + d) % 8
        return ((other // 2) * 16 + z * 2 + other % 2, feat)

    def signal(sem, peer):
        pl.semaphore_signal(sem, inc=1, device_id=peer, device_id_type=MESH)

    barrier = pltpu.get_barrier_semaphore()
    greeted = [ring4, z_peer4, z_peer2, z_peer1]
    greeted += [x_peer(d) for d in range(1, 4)] + [group_peer(d) for d in range(1, 8)]
    for peer in greeted:
        signal(barrier, peer)

    iota16 = lax.broadcasted_iota(jnp.int32, (16, LANE_BLOCK), 0)
    iota32 = lax.broadcasted_iota(jnp.int32, (32, LANE_BLOCK), 0)
    one, zero = jnp.float32(1.0), jnp.float32(0.0)

    for load in loads:
        load.wait()

    def prepare(i, side_sums):
        at = pl.ds(pl.multiple_of(i * LANE_BLOCK, LANE_BLOCK), LANE_BLOCK)
        expo = jnp.exp(logits_ref[:, at])
        prob = expo / jnp.sum(expo, axis=0, keepdims=True)
        target = jnp.where(iota32 == labels_ref[:, at], one, zero)
        grad = (prob - target).astype(jnp.bfloat16).astype(jnp.float32)
        hess = (prob * (1.0 - prob)).astype(jnp.bfloat16).astype(jnp.float32)
        both = jnp.concatenate([grad, hess], axis=0)
        node = nodes_ref[:, at]
        row_feature = jnp.zeros_like(node)
        row_bin = jnp.zeros_like(node)
        row_missing = jnp.zeros_like(node)
        for n in range(8):
            here = node == n
            masked[n * 64 : (n + 1) * 64, at] = jnp.where(here, both, zero).astype(jnp.bfloat16)
            row_feature = jnp.where(here, feature_ref[n], row_feature)
            row_bin = jnp.where(here, bin_ref[n], row_bin)
            row_missing = jnp.where(here, missing_ref[n], row_missing)
        column = row_feature - feat * 32
        owned = (column >= 0) & (column < 32)
        code = jnp.sum(
            jnp.where(iota32 == column, codes_ref[:, at].astype(jnp.float32), zero),
            axis=0,
            keepdims=True,
        ).astype(jnp.int32)
        left = (code < row_bin) | ((code == BINS - 1) & (row_missing == 1))
        right = jnp.where(left, 0, 1)
        flag_buf[x, :, at] = jnp.where(owned, right, 0).astype(jnp.float32)
        slot = jnp.where(owned, node * 2 + right, -1)
        slot_hot = jnp.where(iota16 == slot, one, zero).astype(jnp.bfloat16)
        return side_sums + lax.dot_general(
            slot_hot, both.astype(jnp.bfloat16), NT, preferred_element_type=jnp.float32
        )

    side_sums = lax.fori_loop(
        0, rows // LANE_BLOCK, prepare, jnp.zeros((16, 64), jnp.float32)
    )
    x_buf[x] = jnp.concatenate([side_sums, jnp.zeros((16, 64), jnp.float32)], axis=1)

    def remote(src, dst, send, recv, peer):
        return pltpu.make_async_remote_copy(
            src_ref=src,
            dst_ref=dst,
            send_sem=send,
            recv_sem=recv,
            device_id=peer,
            device_id_type=MESH,
        )

    def exchange(buf, send, recv, mine, count, peer):
        def copy(d, slot):
            return remote(buf.at[slot], buf.at[slot], send.at[d - 1], recv.at[slot], peer(d))

        def start():
            for d in range(1, count):
                copy(d, mine).start()

        def arrive():
            for d in range(1, count):
                copy(d, (mine + d) % count).wait_recv()

        def finish():
            for d in range(1, count):
                copy(d, mine).wait_send()

        return start, arrive, finish

    flags = exchange(flag_buf, flag_send, flag_recv, x, 4, x_peer)
    along_x = exchange(x_buf, x_send, x_recv, x, 4, x_peer)
    in_group = exchange(group_buf, group_send, group_recv, group, 8, group_peer)
    pair_peers = (z_peer1, z_peer2, z_peer4, far_peer)

    def pair_copy(i):
        return remote(
            pair_buf.at[i, 0], pair_buf.at[i, 1], pair_send.at[i], pair_recv.at[i], pair_peers[i]
        )

    far_copy = remote(far_flag.at[0], far_flag.at[1], far_send.at[0], far_recv.at[0], far_peer)

    def total(buf, count):
        sums = buf[0]
        for i in range(1, count):
            sums = sums + buf[i]
        return sums

    def after_x():
        along_x[1]()
        group_buf[group] = total(x_buf, 4)
        in_group[0]()

    def after_group():
        in_group[1]()
        pair_buf[0, 0] = total(group_buf, 8)
        pair_copy(0).start()

    def after_pair(i):
        pair_copy(i).wait_recv()
        pair_buf[i + 1, 0] = pair_buf[i, 0] + pair_buf[i, 1]
        pair_copy(i + 1).start()

    def core_copy(k):
        return remote(
            hist.at[2 * k], core_buf.at[k], core_send.at[k], core_recv.at[k], core_peer
        )

    first_y = (ya, yb)
    second_y = (yb, ya)

    def part_of(k, dest, colour):
        return hist.at[2 * k + 1, :, pl.ds(2 * dest, 2), pl.ds(32 * colour, 32)]

    def y1_copy(k, colour, part):
        dest = first_y[colour] if part else yc
        return remote(
            part_of(k, dest, colour),
            y1_buf.at[k, colour, part],
            y1_send.at[k, colour, part],
            y1_recv.at[k, colour, part],
            at_y(first_y[colour]),
        )

    def y2_copy(k, colour):
        dest = second_y[colour]
        return remote(
            part_of(k, dest, colour),
            y2_buf.at[k, colour],
            y2_send.at[k, colour],
            y2_recv.at[k, colour],
            at_y(dest),
        )

    def z1_copy(k, colour):
        return remote(
            part_of(k, y, colour),
            z1_buf.at[k // 2, colour],
            z1_send.at[k // 2, colour],
            z1_recv.at[k // 2, colour],
            z_peer1,
        )

    def direct_copy(k, colour, d):
        other = (quad + d) % 4
        return remote(
            hist.at[2 * k + 1, other % 2, 2 * y + other // 2, pl.ds(32 * colour, 32)],
            direct_buf.at[k // 2, colour, d - 1],
            direct_send.at[k // 2, colour, d - 1],
            direct_recv.at[k // 2, colour, d - 1],
            at_z(other * 2 + z0),
        )

    iota64 = lax.broadcasted_iota(jnp.int32, (64, rows), 0)

    def after_core(k):
        core_copy(k).wait_recv()
        hist[2 * k + 1] = hist[2 * k + 1] + core_buf[k]

    def send_y1(k):
        for part in range(2):
            for colour in range(2):
                y1_copy(k, colour, part).start()

    def step(s, carry):
        k = s // 2
        side = s % 2
        half, pair = k % 2, k // 2
        owner = side * core + (1 - side) * (1 - core)
        base = half * 8 + owner * 4 + pair * 2
        for high in range(2):
            for low in range(2):
                code = codes_ref[pl.ds(base + 16 * high + low, 1), :]
                start = (high * 2 + low) * 64
                hot[start : start + 64, :] = jnp.where(code == iota64, one, zero).astype(
                    jnp.bfloat16
                )
        out = lax.dot_general(masked[...], hot[...], NT, preferred_element_type=jnp.float32)
        for high in range(2):
            for n in range(8):
                hist[s, high, n] = out[n * 64 : (n + 1) * 64, high * 128 : (high + 1) * 128]

        @pl.when(s == 0)
        def _():
            pl.semaphore_wait(barrier, len(greeted))
            signal(vouch4, ring4)
            signal(vouch4, z_peer4)
            signal(vouch2, z_peer2)

        @pl.when(side == 0)
        def _():
            core_copy(k).start()

        @pl.when(s == 0)
        def _():
            along_x[0]()
            flags[0]()

        @pl.when((side == 0) & (k > 0))
        def _():
            after_core(k - 1)

        @pl.when((side == 0) & (k > 0) & (k < 3))
        def _():
            send_y1(k - 1)

        @pl.when(s == 3)
        def _():
            after_x()

        @pl.when(s == 7)
        def _():
            after_group()

        return carry

    lax.fori_loop(0, 8, step, 0)

    def add_part(k, dest, colour, incoming):
        at = pl.ds(2 * dest, 2)
        lines = slice(32 * colour, 32 * colour + 32)
        hist[2 * k + 1, :, at, lines] = hist[2 * k + 1, :, at, lines] + incoming

    def after_y1(k):
        for colour in range(2):
            y1_copy(k, colour, 0).wait_recv()
            add_part(k, second_y[colour], colour, y1_buf[k, colour, 0])
            y2_copy(k, colour).start()
        for colour in range(2):
            y1_copy(k, colour, 1).wait_recv()
            add_part(k, y, colour, y1_buf[k, colour, 1])

    def after_y2(k):
        for colour in range(2):
            y2_copy(k, colour).wait_recv()
            add_part(k, y, colour, y2_buf[k, colour])

            @pl.when(z0 != k % 2)
            def _():
                z1_copy(k, colour).start()

    def after_z1(k):
        @pl.when(z0 == k % 2)
        def _():
            for colour in range(2):
                z1_copy(k, colour).wait_recv()
                add_part(k, y, colour, z1_buf[k // 2, colour])
                for d in (2, 1, 3):
                    direct_copy(k, colour, d).start()

    after_y1(0)
    send_y1(2)
    after_core(3)
    pl.semaphore_wait(vouch4, 2)
    pl.semaphore_wait(vouch2, 1)
    flags[1]()
    far_flag[0] = total(flag_buf, 4)
    far_copy.start()
    after_y1(1)
    send_y1(3)
    after_pair(0)
    after_y2(0)
    after_y1(2)
    after_pair(1)
    after_y2(1)
    after_z1(0)
    after_y1(3)
    after_y2(2)
    after_pair(2)
    after_z1(1)
    after_y2(3)
    after_z1(2)
    after_z1(3)

    pair_copy(3).wait_recv()
    sums_t = jnp.transpose(pair_buf[3, 0] + pair_buf[3, 1])[:64, :]
    leaves_t = -sums_t[:32] / (sums_t[32:] + reg_lambda)
    leaves = jnp.transpose(leaves_t)
    for n in range(8):
        leaves_ref[n] = leaves[2 * n : 2 * n + 2, :]
    far_copy.wait_recv()

    def update(i, carry):
        at = pl.ds(pl.multiple_of(i * LANE_BLOCK, LANE_BLOCK), LANE_BLOCK)
        count = far_flag[0, :, at] + far_flag[1, :, at]
        slot = nodes_ref[:, at] * 2 + jnp.where(count > 0.5, 1, 0)
        slot_hot = jnp.where(iota16 == slot, one, zero).astype(jnp.bfloat16)
        new_ref[:, at] = logits_ref[:, at] + step_size * exact_dot(leaves_t, slot_hot, NN)
        return carry

    lax.fori_loop(0, rows // LANE_BLOCK, update, 0)
    stores[0].start()
    stores[1].start()

    lane_in = lax.broadcasted_iota(jnp.int32, (128, 128), 0)
    lane_out = lax.broadcasted_iota(jnp.int32, (128, 128), 1)
    same = (lane_in // BINS) == (lane_out // BINS)
    bin_in, bin_out = lane_in % BINS, lane_out % BINS
    as_weights = lambda mask: jnp.where(mask, one, zero).astype(jnp.bfloat16)
    lower = as_weights(same & (bin_in < bin_out) & (bin_in < BINS - 1))
    every = as_weights(same)
    last = as_weights(same & (bin_in == BINS - 1))
    lane = lax.broadcasted_iota(jnp.int32, (1, 128), 1)
    for pair in range(2):
        k = 2 * pair + z0
        parts = []
        for colour in range(2):
            part = hist[2 * k + 1, z1, 2 * y + z2, 32 * colour : 32 * colour + 32]
            for d in (2, 1, 3):
                direct_copy(k, colour, d).wait_recv()
                part = part + direct_buf[pair, colour, d - 1]
            parts.append(part)
        owned = jnp.concatenate(parts, axis=0)
        left_base = exact_dot(owned, lower, NN)
        node_total = exact_dot(owned, every, NN)
        left_miss = left_base + exact_dot(owned, last, NN)
        parent = ratio(node_total)
        gain_left = (ratio(left_miss) + ratio(node_total - left_miss) - parent) / 64.0
        gain_right = (ratio(left_base) + ratio(node_total - left_base) - parent) / 64.0
        gain_ref[0, 2 * pair : 2 * pair + 1, :] = jnp.where(
            lane < BINS, gain_left, pltpu.roll(gain_right, BINS, 1)
        )
        gain_ref[0, 2 * pair + 1 : 2 * pair + 2, :] = jnp.where(
            lane < BINS, pltpu.roll(gain_left, BINS, 1), gain_right
        )

    stores[2].start()
    for stage in (flags, along_x, in_group):
        stage[2]()
    far_copy.wait_send()
    for i in range(4):
        pair_copy(i).wait_send()
    for k in range(4):
        core_copy(k).wait_send()
        for colour in range(2):
            y1_copy(k, colour, 0).wait_send()
            y1_copy(k, colour, 1).wait_send()
            y2_copy(k, colour).wait_send()
    for pair in range(2):
        for colour in range(2):
            z1_copy(2 * pair + 1 - z0, colour).wait_send()
            for d in (1, 2, 3):
                direct_copy(2 * pair + z0, colour, d).wait_send()
    for store in stores:
        store.wait()


def move(new_ref, gain_ref, leaves_ref, new_out, gain_out, leaves_out, new_held, gain_held, leaves_held, sems):
    width = new_ref.shape[1] // 4
    parts = [(leaves_ref, leaves_held, leaves_out), (gain_ref, gain_held, gain_out)]
    for i in range(4):
        at = (slice(None), pl.ds(i * width, width))
        parts.append((new_ref.at[at], new_held.at[at], new_out.at[at]))
    loads = [pltpu.make_async_copy(a, b, sems.at[0, i]) for i, (a, b, _) in enumerate(parts)]
    stores = [pltpu.make_async_copy(b, c, sems.at[1, i]) for i, (_, b, c) in enumerate(parts)]
    for load in loads:
        load.start()
    for load, store in zip(loads, stores):
        load.wait()
        store.start()
    for store in stores:
        store.wait()


def local(logits, labels, node_ids, bin_codes, split_feature, split_bin, split_missing):
    rows = logits.shape[0]
    f32, i32 = jnp.float32, jnp.int32
    hbm = pl.BlockSpec(memory_space=pl.ANY)
    dma = pltpu.SemaphoreType.DMA
    out_shape = (
        jax.ShapeDtypeStruct((32, rows), f32),
        jax.ShapeDtypeStruct((1, 4, 128), f32),
        jax.ShapeDtypeStruct((8, 2, 32), f32),
    )
    results = pl.pallas_call(
        kernel,
        out_shape=out_shape,
        in_specs=[hbm] * 7,
        out_specs=(hbm, hbm, hbm),
        scratch_shapes=[
            pltpu.VMEM((32, rows), f32),
            pltpu.VMEM((1, 4, 128), f32),
            pltpu.VMEM((8, 2, 32), f32),
            pltpu.SMEM((8,), i32),
            pltpu.SMEM((8,), i32),
            pltpu.SMEM((8,), i32),
            pltpu.VMEM((32, rows), f32),
            pltpu.VMEM((1, rows), i32),
            pltpu.VMEM((1, rows), i32),
            pltpu.VMEM((32, rows), i32),
            pltpu.VMEM((512, rows), jnp.bfloat16),
            pltpu.VMEM((256, rows), jnp.bfloat16),
            pltpu.VMEM((8, 2, 8, 64, 128), f32),
            pltpu.VMEM((4, 2, 8, 64, 128), f32),
            pltpu.VMEM((4, 2, 2, 2, 2, 32, 128), f32),
            pltpu.VMEM((4, 2, 2, 2, 32, 128), f32),
            pltpu.VMEM((2, 2, 2, 2, 32, 128), f32),
            pltpu.VMEM((2, 2, 3, 32, 128), f32),
            pltpu.VMEM((4, 1, rows), f32),
            pltpu.VMEM((2, 1, rows), f32),
            pltpu.VMEM((4, 16, 128), f32),
            pltpu.VMEM((8, 16, 128), f32),
            pltpu.VMEM((4, 2, 16, 128), f32),
            dma((7,)),
            dma((3,)),
            dma((4,)),
            dma((4,)),
            dma((4, 2, 2)),
            dma((4, 2, 2)),
            dma((4, 2)),
            dma((4, 2)),
            dma((2, 2)),
            dma((2, 2)),
            dma((2, 2, 3)),
            dma((2, 2, 3)),
            dma((3,)),
            dma((4,)),
            dma((1,)),
            dma((1,)),
            dma((3,)),
            dma((4,)),
            dma((7,)),
            dma((8,)),
            dma((4,)),
            dma((4,)),
            pltpu.SemaphoreType.REGULAR,
            pltpu.SemaphoreType.REGULAR,
        ],
        compiler_params=pltpu.CompilerParams(
            collective_id=0, has_side_effects=True, vmem_limit_bytes=56 * 1024 * 1024
        ),
    )(
        split_feature,
        split_bin,
        split_missing,
        logits.T,
        labels.reshape(1, rows),
        node_ids.reshape(1, rows),
        bin_codes.T,
    )
    new_t, gains, leaves = pl.pallas_call(
        move,
        out_shape=out_shape,
        in_specs=[hbm] * 3,
        out_specs=(hbm, hbm, hbm),
        scratch_shapes=[
            pltpu.VMEM((32, rows), f32),
            pltpu.VMEM((1, 4, 128), f32),
            pltpu.VMEM((8, 2, 32), f32),
            dma((2, 6)),
        ],
    )(*results)
    return new_t.T, gains, leaves


def solution(mesh):
    return jax.shard_map(
        local,
        mesh=mesh,
        in_specs=(P("rows", None), P("rows"), P("rows"), P("rows", "feat"), P(), P(), P()),
        out_specs=(P("rows", None), P("rows", "feat", None), P()),
        check_vma=False,
    )
```

```python
import jax
import jax.numpy as jnp
from jax import lax
from jax.experimental import pallas as pl
from jax.experimental.pallas import tpu as pltpu
from jax.sharding import PartitionSpec as P

BINS = 64
MESH = pl.DeviceIdType.MESH
reg_lambda = 1.0
step_size = 0.3
LANE_BLOCK = 512
NT = (((1,), (1,)), ((), ()))
NN = (((1,), (0,)), ((), ()))


def split3(x):
    hi = x.astype(jnp.bfloat16)
    rest = x - hi.astype(jnp.float32)
    mid = rest.astype(jnp.bfloat16)
    low = (rest - mid.astype(jnp.float32)).astype(jnp.bfloat16)
    return hi, mid, low


def exact_dot(x, weights, dims):
    hi, mid, low = split3(x)
    dot = lambda part: lax.dot_general(part, weights, dims, preferred_element_type=jnp.float32)
    return dot(hi) + (dot(mid) + dot(low))


def ratio(sums):
    grad_part = sums[:32]
    hess_part = sums[32:]
    return jnp.sum(grad_part * grad_part / (hess_part + reg_lambda), axis=0, keepdims=True)


def kernel(
    feature_hbm,
    bin_hbm,
    missing_hbm,
    logits_hbm,
    labels_hbm,
    nodes_hbm,
    codes_hbm,
    new_hbm,
    gain_hbm,
    leaves_hbm,
    new_ref,
    gain_ref,
    leaves_ref,
    feature_ref,
    bin_ref,
    missing_ref,
    logits_ref,
    labels_ref,
    nodes_ref,
    codes_ref,
    masked,
    hot,
    hist,
    core_buf,
    y1_buf,
    y2_buf,
    z1_buf,
    direct_buf,
    flag_buf,
    far_flag,
    x_buf,
    group_buf,
    pair_buf,
    wide_buf,
    load_sem,
    store_sem,
    core_send,
    core_recv,
    y1_send,
    y1_recv,
    y2_send,
    y2_recv,
    z1_send,
    z1_recv,
    direct_send,
    direct_recv,
    flag_send,
    flag_recv,
    far_send,
    far_recv,
    x_send,
    x_recv,
    group_send,
    group_recv,
    pair_send,
    pair_recv,
    wide_send,
    wide_recv,
    vouch4,
    vouch2,
):
    rows = logits_ref.shape[1]
    row = lax.axis_index("rows")
    feat = lax.axis_index("feat")
    core = row % 2
    z = (row // 2) % 8
    y = row // 16
    x, z_hi = feat // 2, feat % 2
    z0, z1, z2 = z % 2, (z // 2) % 2, z // 4
    quad = z // 2
    group = (y * 2 + core) * 2 + z0
    wide = z_hi * 2 + z2
    ya = y + 1 - 2 * (y % 2)
    yb = 3 - y
    yc = 3 - ya

    loads = [
        pltpu.make_async_copy(src, dst, load_sem.at[i])
        for i, (src, dst) in enumerate(
            (
                (logits_hbm, logits_ref),
                (labels_hbm, labels_ref),
                (nodes_hbm, nodes_ref),
                (codes_hbm, codes_ref),
                (feature_hbm, feature_ref),
                (bin_hbm, bin_ref),
                (missing_hbm, missing_ref),
            )
        )
    ]
    for load in loads:
        load.start()
    stores = [
        pltpu.make_async_copy(src, dst, store_sem.at[i])
        for i, (src, dst) in enumerate(
            ((new_ref, new_hbm), (leaves_ref, leaves_hbm), (gain_ref, gain_hbm))
        )
    ]

    def at_y(other):
        return (other * 16 + z * 2 + core, feat)

    def at_z(other):
        return (y * 16 + other * 2 + core, feat)

    core_peer = (row + 1 - 2 * core, feat)
    z_peer1 = at_z(z + 1 - 2 * z0)
    z_peer2 = at_z(z + 2 - 4 * z1)
    z_peer4 = at_z(z + 4 - 8 * z2)
    far_peer = (row, x * 2 + 1 - z_hi)
    ring4 = (y * 16 + ((z + 4) % 8) * 2 + core, x * 2 + 1 - z_hi)

    def x_peer(d):
        return (row, ((x + d) % 4) * 2 + z_hi)

    def group_peer(d):
        other = (group + d) % 16
        return ((other // 4) * 16 + (z - z0 + other % 2) * 2 + (other // 2) % 2, feat)

    def wide_peer(d):
        other = (wide + d) % 4
        return (y * 16 + (z % 4 + 4 * (other % 2)) * 2 + core, x * 2 + other // 2)

    def signal(sem, peer):
        pl.semaphore_signal(sem, inc=1, device_id=peer, device_id_type=MESH)

    barrier = pltpu.get_barrier_semaphore()
    greeted = [ring4, z_peer4, z_peer2]
    greeted += [x_peer(d) for d in range(1, 4)] + [group_peer(d) for d in range(1, 16)]
    for peer in greeted:
        signal(barrier, peer)

    iota16 = lax.broadcasted_iota(jnp.int32, (16, LANE_BLOCK), 0)
    iota32 = lax.broadcasted_iota(jnp.int32, (32, LANE_BLOCK), 0)
    one, zero = jnp.float32(1.0), jnp.float32(0.0)

    for load in loads:
        load.wait()

    def prepare(i, side_sums):
        at = pl.ds(pl.multiple_of(i * LANE_BLOCK, LANE_BLOCK), LANE_BLOCK)
        expo = jnp.exp(logits_ref[:, at])
        prob = expo / jnp.sum(expo, axis=0, keepdims=True)
        target = jnp.where(iota32 == labels_ref[:, at], one, zero)
        grad = (prob - target).astype(jnp.bfloat16).astype(jnp.float32)
        hess = (prob * (1.0 - prob)).astype(jnp.bfloat16).astype(jnp.float32)
        both = jnp.concatenate([grad, hess], axis=0)
        node = nodes_ref[:, at]
        row_feature = jnp.zeros_like(node)
        row_bin = jnp.zeros_like(node)
        row_missing = jnp.zeros_like(node)
        for n in range(8):
            here = node == n
            masked[n * 64 : (n + 1) * 64, at] = jnp.where(here, both, zero).astype(jnp.bfloat16)
            row_feature = jnp.where(here, feature_ref[n], row_feature)
            row_bin = jnp.where(here, bin_ref[n], row_bin)
            row_missing = jnp.where(here, missing_ref[n], row_missing)
        column = row_feature - feat * 32
        owned = (column >= 0) & (column < 32)
        code = jnp.sum(
            jnp.where(iota32 == column, codes_ref[:, at].astype(jnp.float32), zero),
            axis=0,
            keepdims=True,
        ).astype(jnp.int32)
        left = (code < row_bin) | ((code == BINS - 1) & (row_missing == 1))
        right = jnp.where(left, 0, 1)
        flag_buf[x, :, at] = jnp.where(owned, right, 0).astype(jnp.float32)
        slot = jnp.where(owned, node * 2 + right, -1)
        slot_hot = jnp.where(iota16 == slot, one, zero).astype(jnp.bfloat16)
        return side_sums + lax.dot_general(
            slot_hot, both.astype(jnp.bfloat16), NT, preferred_element_type=jnp.float32
        )

    side_sums = lax.fori_loop(
        0, rows // LANE_BLOCK, prepare, jnp.zeros((16, 64), jnp.float32)
    )
    x_buf[x] = jnp.concatenate([side_sums[:8], side_sums[8:]], axis=1)

    def remote(src, dst, send, recv, peer):
        return pltpu.make_async_remote_copy(
            src_ref=src,
            dst_ref=dst,
            send_sem=send,
            recv_sem=recv,
            device_id=peer,
            device_id_type=MESH,
        )

    def exchange(buf, send, recv, mine, count, peer):
        def copy(d, slot):
            return remote(buf.at[slot], buf.at[slot], send.at[d - 1], recv.at[slot], peer(d))

        def start():
            for d in range(1, count):
                copy(d, mine).start()

        def arrive():
            for d in range(1, count):
                copy(d, (mine + d) % count).wait_recv()

        def finish():
            for d in range(1, count):
                copy(d, mine).wait_send()

        return start, arrive, finish

    flags = exchange(flag_buf, flag_send, flag_recv, x, 4, x_peer)
    along_x = exchange(x_buf, x_send, x_recv, x, 4, x_peer)
    in_group = exchange(group_buf, group_send, group_recv, group, 16, group_peer)
    along_z = exchange(wide_buf, wide_send, wide_recv, wide, 4, wide_peer)
    pair_copy = remote(
        pair_buf.at[0], pair_buf.at[1], pair_send.at[0], pair_recv.at[0], z_peer2
    )
    far_copy = remote(far_flag.at[0], far_flag.at[1], far_send.at[0], far_recv.at[0], far_peer)

    def total(buf, count):
        sums = buf[0]
        for i in range(1, count):
            sums = sums + buf[i]
        return sums

    def after_x():
        along_x[1]()
        group_buf[group] = total(x_buf, 4)
        in_group[0]()

    def after_group():
        in_group[1]()
        pair_buf[0] = total(group_buf, 16)
        pair_copy.start()

    def after_pair():
        pair_copy.wait_recv()
        wide_buf[wide] = pair_buf[0] + pair_buf[1]
        along_z[0]()

    def core_copy(k):
        return remote(
            hist.at[2 * k], core_buf.at[k], core_send.at[k], core_recv.at[k], core_peer
        )

    first_y = (ya, yb)
    second_y = (yb, ya)

    def part_of(u, dest, colour):
        lines = pl.ds(32 * (u % 2) + 16 * colour, 16)
        return hist.at[2 * (u // 2) + 1, :, pl.ds(2 * dest, 2), lines]

    def y1_copy(u, colour, part):
        dest = first_y[colour] if part else yc
        return remote(
            part_of(u, dest, colour),
            y1_buf.at[u, colour, part],
            y1_send.at[u, colour, part],
            y1_recv.at[u, colour, part],
            at_y(first_y[colour]),
        )

    def y2_copy(u, colour):
        dest = second_y[colour]
        return remote(
            part_of(u, dest, colour),
            y2_buf.at[u, colour],
            y2_send.at[u, colour],
            y2_recv.at[u, colour],
            at_y(dest),
        )

    def z1_copy(k, colour):
        return remote(
            hist.at[2 * k + 1, :, pl.ds(2 * y, 2), pl.ds(32 * colour, 32)],
            z1_buf.at[k // 2, colour],
            z1_send.at[k // 2, colour],
            z1_recv.at[k // 2, colour],
            z_peer1,
        )

    def direct_copy(k, colour, d):
        other = (quad + d) % 4
        return remote(
            hist.at[2 * k + 1, other % 2, 2 * y + other // 2, pl.ds(32 * colour, 32)],
            direct_buf.at[k // 2, colour, d - 1],
            direct_send.at[k // 2, colour, d - 1],
            direct_recv.at[k // 2, colour, d - 1],
            at_z(other * 2 + z0),
        )

    iota64 = lax.broadcasted_iota(jnp.int32, (64, rows), 0)

    def after_core(k):
        core_copy(k).wait_recv()
        hist[2 * k + 1] = hist[2 * k + 1] + core_buf[k]

    def send_y1(u):
        for part in range(2):
            for colour in range(2):
                y1_copy(u, colour, part).start()

    def add_lines(k, dest, first, count, incoming):
        at = (2 * k + 1, slice(None), pl.ds(2 * dest, 2), slice(first, first + count))
        hist[at] = hist[at] + incoming

    def add_part(u, dest, colour, incoming):
        add_lines(u // 2, dest, 32 * (u % 2) + 16 * colour, 16, incoming)

    def after_y1(u):
        for colour in range(2):
            y1_copy(u, colour, 0).wait_recv()
            add_part(u, second_y[colour], colour, y1_buf[u, colour, 0])
            y2_copy(u, colour).start()
        for colour in range(2):
            y1_copy(u, colour, 1).wait_recv()
            add_part(u, y, colour, y1_buf[u, colour, 1])

    def after_y2(u):
        for colour in range(2):
            y2_copy(u, colour).wait_recv()
            add_part(u, y, colour, y2_buf[u, colour])

        @pl.when(z0 != (u // 2) % 2)
        def _():
            z1_copy(u // 2, u % 2).start()

    def after_z1(u):
        k, half = u // 2, u % 2

        @pl.when(z0 == k % 2)
        def _():
            z1_copy(k, half).wait_recv()
            add_lines(k, y, 32 * half, 32, z1_buf[k // 2, half])
            for d in (2, 1, 3):
                direct_copy(k, half, d).start()

    def step(s, carry):
        k = s // 2
        side = s % 2
        half, pair = k % 2, k // 2
        owner = side * core + (1 - side) * (1 - core)
        base = half * 8 + owner * 4 + pair * 2
        for high in range(2):
            for low in range(2):
                code = codes_ref[pl.ds(base + 16 * high + low, 1), :]
                start = (high * 2 + low) * 64
                hot[start : start + 64, :] = jnp.where(code == iota64, one, zero).astype(
                    jnp.bfloat16
                )
        out = lax.dot_general(masked[...], hot[...], NT, preferred_element_type=jnp.float32)
        for high in range(2):
            for n in range(8):
                hist[s, high, n] = out[n * 64 : (n + 1) * 64, high * 128 : (high + 1) * 128]

        @pl.when(s == 0)
        def _():
            pl.semaphore_wait(barrier, len(greeted))
            signal(vouch4, ring4)
            signal(vouch4, z_peer4)
            signal(vouch2, z_peer2)

        @pl.when(side == 0)
        def _():
            core_copy(k).start()

        @pl.when(s == 0)
        def _():
            along_x[0]()
            flags[0]()

        @pl.when((side == 0) & (k > 0))
        def _():
            after_core(k - 1)

        @pl.when(s == 2)
        def _():
            send_y1(0)
            send_y1(1)

        @pl.when(s == 3)
        def _():
            after_x()

        @pl.when(s == 4)
        def _():
            send_y1(2)

        @pl.when(s == 5)
        def _():
            after_y1(0)
            send_y1(3)

        @pl.when(s == 6)
        def _():
            after_y1(1)
            send_y1(4)

        @pl.when(s == 7)
        def _():
            after_group()

        return carry

    lax.fori_loop(0, 8, step, 0)

    for u in range(2, 8):
        after_y1(u)
        if u == 2:
            after_core(3)
        if u + 3 < 8:
            send_y1(u + 3)
        after_y2(u - 2)
        if u == 2:
            pl.semaphore_wait(vouch4, 2)
            pl.semaphore_wait(vouch2, 1)
            flags[1]()
            far_flag[0] = total(flag_buf, 4)
            far_copy.start()
        if u == 3:
            after_pair()
        if u >= 4:
            after_z1(u - 4)
    after_y2(6)
    after_z1(4)
    after_y2(7)
    after_z1(5)
    after_z1(6)
    after_z1(7)

    along_z[1]()
    sums = total(wide_buf, 4)
    sums = jnp.concatenate([sums, pltpu.roll(sums, 64, 1)], axis=0)
    sums_t = jnp.transpose(sums)[:64, :]
    leaves_t = -sums_t[:32] / (sums_t[32:] + reg_lambda)
    leaves = jnp.transpose(leaves_t)
    for n in range(8):
        leaves_ref[n] = leaves[2 * n : 2 * n + 2, :]
    far_copy.wait_recv()

    def update(i, carry):
        at = pl.ds(pl.multiple_of(i * LANE_BLOCK, LANE_BLOCK), LANE_BLOCK)
        count = far_flag[0, :, at] + far_flag[1, :, at]
        slot = nodes_ref[:, at] * 2 + jnp.where(count > 0.5, 1, 0)
        slot_hot = jnp.where(iota16 == slot, one, zero).astype(jnp.bfloat16)
        new_ref[:, at] = logits_ref[:, at] + step_size * exact_dot(leaves_t, slot_hot, NN)
        return carry

    lax.fori_loop(0, rows // LANE_BLOCK, update, 0)
    stores[0].start()
    stores[1].start()

    lane_in = lax.broadcasted_iota(jnp.int32, (128, 128), 0)
    lane_out = lax.broadcasted_iota(jnp.int32, (128, 128), 1)
    same = (lane_in // BINS) == (lane_out // BINS)
    bin_in, bin_out = lane_in % BINS, lane_out % BINS
    as_weights = lambda mask: jnp.where(mask, one, zero).astype(jnp.bfloat16)
    lower = as_weights(same & (bin_in < bin_out) & (bin_in < BINS - 1))
    every = as_weights(same)
    last = as_weights(same & (bin_in == BINS - 1))
    lane = lax.broadcasted_iota(jnp.int32, (1, 128), 1)
    for pair in range(2):
        k = 2 * pair + z0
        parts = []
        for colour in range(2):
            part = hist[2 * k + 1, z1, 2 * y + z2, 32 * colour : 32 * colour + 32]
            for d in (2, 1, 3):
                direct_copy(k, colour, d).wait_recv()
                part = part + direct_buf[pair, colour, d - 1]
            parts.append(part)
        owned = jnp.concatenate(parts, axis=0)
        left_base = exact_dot(owned, lower, NN)
        node_total = exact_dot(owned, every, NN)
        left_miss = left_base + exact_dot(owned, last, NN)
        parent = ratio(node_total)
        gain_left = (ratio(left_miss) + ratio(node_total - left_miss) - parent) / 64.0
        gain_right = (ratio(left_base) + ratio(node_total - left_base) - parent) / 64.0
        gain_ref[0, 2 * pair : 2 * pair + 1, :] = jnp.where(
            lane < BINS, gain_left, pltpu.roll(gain_right, BINS, 1)
        )
        gain_ref[0, 2 * pair + 1 : 2 * pair + 2, :] = jnp.where(
            lane < BINS, pltpu.roll(gain_left, BINS, 1), gain_right
        )

    stores[2].start()
    for stage in (flags, along_x, in_group, along_z):
        stage[2]()
    far_copy.wait_send()
    pair_copy.wait_send()
    for k in range(4):
        core_copy(k).wait_send()
    for u in range(8):
        for colour in range(2):
            y1_copy(u, colour, 0).wait_send()
            y1_copy(u, colour, 1).wait_send()
            y2_copy(u, colour).wait_send()
    for pair in range(2):
        for colour in range(2):
            z1_copy(2 * pair + 1 - z0, colour).wait_send()
            for d in (1, 2, 3):
                direct_copy(2 * pair + z0, colour, d).wait_send()
    for store in stores:
        store.wait()


def move(new_ref, gain_ref, leaves_ref, new_out, gain_out, leaves_out, new_held, gain_held, leaves_held, sems):
    width = new_ref.shape[1] // 4
    parts = [(leaves_ref, leaves_held, leaves_out), (gain_ref, gain_held, gain_out)]
    for i in range(4):
        at = (slice(None), pl.ds(i * width, width))
        parts.append((new_ref.at[at], new_held.at[at], new_out.at[at]))
    loads = [pltpu.make_async_copy(a, b, sems.at[0, i]) for i, (a, b, _) in enumerate(parts)]
    stores = [pltpu.make_async_copy(b, c, sems.at[1, i]) for i, (_, b, c) in enumerate(parts)]
    for load in loads:
        load.start()
    for load, store in zip(loads, stores):
        load.wait()
        store.start()
    for store in stores:
        store.wait()


def local(logits, labels, node_ids, bin_codes, split_feature, split_bin, split_missing):
    rows = logits.shape[0]
    f32, i32 = jnp.float32, jnp.int32
    hbm = pl.BlockSpec(memory_space=pl.ANY)
    dma = pltpu.SemaphoreType.DMA
    out_shape = (
        jax.ShapeDtypeStruct((32, rows), f32),
        jax.ShapeDtypeStruct((1, 4, 128), f32),
        jax.ShapeDtypeStruct((8, 2, 32), f32),
    )
    results = pl.pallas_call(
        kernel,
        out_shape=out_shape,
        in_specs=[hbm] * 7,
        out_specs=(hbm, hbm, hbm),
        scratch_shapes=[
            pltpu.VMEM((32, rows), f32),
            pltpu.VMEM((1, 4, 128), f32),
            pltpu.VMEM((8, 2, 32), f32),
            pltpu.SMEM((8,), i32),
            pltpu.SMEM((8,), i32),
            pltpu.SMEM((8,), i32),
            pltpu.VMEM((32, rows), f32),
            pltpu.VMEM((1, rows), i32),
            pltpu.VMEM((1, rows), i32),
            pltpu.VMEM((32, rows), i32),
            pltpu.VMEM((512, rows), jnp.bfloat16),
            pltpu.VMEM((256, rows), jnp.bfloat16),
            pltpu.VMEM((8, 2, 8, 64, 128), f32),
            pltpu.VMEM((4, 2, 8, 64, 128), f32),
            pltpu.VMEM((8, 2, 2, 2, 2, 16, 128), f32),
            pltpu.VMEM((8, 2, 2, 2, 16, 128), f32),
            pltpu.VMEM((2, 2, 2, 2, 32, 128), f32),
            pltpu.VMEM((2, 2, 3, 32, 128), f32),
            pltpu.VMEM((4, 1, rows), f32),
            pltpu.VMEM((2, 1, rows), f32),
            pltpu.VMEM((4, 8, 128), f32),
            pltpu.VMEM((16, 8, 128), f32),
            pltpu.VMEM((2, 8, 128), f32),
            pltpu.VMEM((4, 8, 128), f32),
            dma((7,)),
            dma((3,)),
            dma((4,)),
            dma((4,)),
            dma((8, 2, 2)),
            dma((8, 2, 2)),
            dma((8, 2)),
            dma((8, 2)),
            dma((2, 2)),
            dma((2, 2)),
            dma((2, 2, 3)),
            dma((2, 2, 3)),
            dma((3,)),
            dma((4,)),
            dma((1,)),
            dma((1,)),
            dma((3,)),
            dma((4,)),
            dma((15,)),
            dma((16,)),
            dma((1,)),
            dma((1,)),
            dma((3,)),
            dma((4,)),
            pltpu.SemaphoreType.REGULAR,
            pltpu.SemaphoreType.REGULAR,
        ],
        compiler_params=pltpu.CompilerParams(
            collective_id=0, has_side_effects=True, vmem_limit_bytes=56 * 1024 * 1024
        ),
    )(
        split_feature,
        split_bin,
        split_missing,
        logits.T,
        labels.reshape(1, rows),
        node_ids.reshape(1, rows),
        bin_codes.T,
    )
    new_t, gains, leaves = pl.pallas_call(
        move,
        out_shape=out_shape,
        in_specs=[hbm] * 3,
        out_specs=(hbm, hbm, hbm),
        scratch_shapes=[
            pltpu.VMEM((32, rows), f32),
            pltpu.VMEM((1, 4, 128), f32),
            pltpu.VMEM((8, 2, 32), f32),
            dma((2, 6)),
        ],
    )(*results)
    return new_t.T, gains, leaves


def solution(mesh):
    return jax.shard_map(
        local,
        mesh=mesh,
        in_specs=(P("rows", None), P("rows"), P("rows"), P("rows", "feat"), P(), P(), P()),
        out_specs=(P("rows", None), P("rows", "feat", None), P()),
        check_vma=False,
    )
```

```python
import jax
import jax.numpy as jnp
from jax import lax
from jax.experimental import pallas as pl
from jax.experimental.pallas import tpu as pltpu
from jax.sharding import PartitionSpec as P

BINS = 64
MESH = pl.DeviceIdType.MESH
reg_lambda = 1.0
step_size = 0.3
LANE_BLOCK = 512
NT = (((1,), (1,)), ((), ()))
NN = (((1,), (0,)), ((), ()))


def split3(x):
    hi = x.astype(jnp.bfloat16)
    rest = x - hi.astype(jnp.float32)
    mid = rest.astype(jnp.bfloat16)
    low = (rest - mid.astype(jnp.float32)).astype(jnp.bfloat16)
    return hi, mid, low


def exact_dot(x, weights, dims):
    hi, mid, low = split3(x)
    dot = lambda part: lax.dot_general(part, weights, dims, preferred_element_type=jnp.float32)
    return dot(hi) + (dot(mid) + dot(low))


def ratio(sums):
    grad_part = sums[:32]
    hess_part = sums[32:]
    return jnp.sum(grad_part * grad_part / (hess_part + reg_lambda), axis=0, keepdims=True)


def kernel(
    feature_hbm,
    bin_hbm,
    missing_hbm,
    logits_hbm,
    labels_hbm,
    nodes_hbm,
    codes_hbm,
    new_hbm,
    gain_hbm,
    leaves_hbm,
    new_ref,
    gain_ref,
    leaves_ref,
    feature_ref,
    bin_ref,
    missing_ref,
    logits_ref,
    labels_ref,
    nodes_ref,
    codes_ref,
    masked,
    hot,
    hist,
    core_buf,
    y1_buf,
    y1_late,
    y2_buf,
    y2_late,
    z1_buf,
    z1_late,
    direct_buf,
    direct_late,
    flag_buf,
    far_flag,
    x_buf,
    group_buf,
    pair_buf,
    wide_buf,
    load_sem,
    store_sem,
    core_send,
    core_recv,
    y1_send,
    y1_recv,
    y2_send,
    y2_recv,
    z1_send,
    z1_recv,
    direct_send,
    direct_recv,
    late_send,
    late_recv,
    flag_send,
    flag_recv,
    far_send,
    far_recv,
    x_send,
    x_recv,
    group_send,
    group_recv,
    pair_send,
    pair_recv,
    wide_send,
    wide_recv,
    vouch4,
    vouch2,
):
    rows = logits_ref.shape[1]
    row = lax.axis_index("rows")
    feat = lax.axis_index("feat")
    core = row % 2
    z = (row // 2) % 8
    y = row // 16
    x, z_hi = feat // 2, feat % 2
    z0, z1, z2 = z % 2, (z // 2) % 2, z // 4
    quad = z // 2
    group = (y * 2 + core) * 2 + z0
    wide = z_hi * 2 + z2
    ya = y + 1 - 2 * (y % 2)
    yb = 3 - y
    yc = 3 - ya

    loads = [
        pltpu.make_async_copy(src, dst, load_sem.at[i])
        for i, (src, dst) in enumerate(
            (
                (logits_hbm, logits_ref),
                (labels_hbm, labels_ref),
                (nodes_hbm, nodes_ref),
                (codes_hbm, codes_ref),
                (feature_hbm, feature_ref),
                (bin_hbm, bin_ref),
                (missing_hbm, missing_ref),
            )
        )
    ]
    for load in loads:
        load.start()
    stores = [
        pltpu.make_async_copy(src, dst, store_sem.at[i])
        for i, (src, dst) in enumerate(
            ((new_ref, new_hbm), (leaves_ref, leaves_hbm), (gain_ref, gain_hbm))
        )
    ]

    def at_y(other):
        return (other * 16 + z * 2 + core, feat)

    def at_z(other):
        return (y * 16 + other * 2 + core, feat)

    core_peer = (row + 1 - 2 * core, feat)
    z_peer1 = at_z(z + 1 - 2 * z0)
    z_peer2 = at_z(z + 2 - 4 * z1)
    z_peer4 = at_z(z + 4 - 8 * z2)
    far_peer = (row, x * 2 + 1 - z_hi)
    ring4 = (y * 16 + ((z + 4) % 8) * 2 + core, x * 2 + 1 - z_hi)

    def x_peer(d):
        return (row, ((x + d) % 4) * 2 + z_hi)

    def group_peer(d):
        other = (group + d) % 16
        return ((other // 4) * 16 + (z - z0 + other % 2) * 2 + (other // 2) % 2, feat)

    def wide_peer(d):
        other = (wide + d) % 4
        return (y * 16 + (z % 4 + 4 * (other % 2)) * 2 + core, x * 2 + other // 2)

    def signal(sem, peer):
        pl.semaphore_signal(sem, inc=1, device_id=peer, device_id_type=MESH)

    barrier = pltpu.get_barrier_semaphore()
    greeted = [ring4, z_peer4, z_peer2]
    greeted += [x_peer(d) for d in range(1, 4)] + [group_peer(d) for d in range(1, 16)]
    for peer in greeted:
        signal(barrier, peer)

    iota16 = lax.broadcasted_iota(jnp.int32, (16, LANE_BLOCK), 0)
    iota32 = lax.broadcasted_iota(jnp.int32, (32, LANE_BLOCK), 0)
    one, zero = jnp.float32(1.0), jnp.float32(0.0)

    for load in loads:
        load.wait()

    def prepare(i, side_sums):
        at = pl.ds(pl.multiple_of(i * LANE_BLOCK, LANE_BLOCK), LANE_BLOCK)
        expo = jnp.exp(logits_ref[:, at])
        prob = expo / jnp.sum(expo, axis=0, keepdims=True)
        target = jnp.where(iota32 == labels_ref[:, at], one, zero)
        grad = (prob - target).astype(jnp.bfloat16).astype(jnp.float32)
        hess = (prob * (1.0 - prob)).astype(jnp.bfloat16).astype(jnp.float32)
        both = jnp.concatenate([grad, hess], axis=0)
        node = nodes_ref[:, at]
        row_feature = jnp.zeros_like(node)
        row_bin = jnp.zeros_like(node)
        row_missing = jnp.zeros_like(node)
        for n in range(8):
            here = node == n
            masked[n * 64 : (n + 1) * 64, at] = jnp.where(here, both, zero).astype(jnp.bfloat16)
            row_feature = jnp.where(here, feature_ref[n], row_feature)
            row_bin = jnp.where(here, bin_ref[n], row_bin)
            row_missing = jnp.where(here, missing_ref[n], row_missing)
        column = row_feature - feat * 32
        owned = (column >= 0) & (column < 32)
        code = jnp.sum(
            jnp.where(iota32 == column, codes_ref[:, at].astype(jnp.float32), zero),
            axis=0,
            keepdims=True,
        ).astype(jnp.int32)
        left = (code < row_bin) | ((code == BINS - 1) & (row_missing == 1))
        right = jnp.where(left, 0, 1)
        flag_buf[x, :, at] = jnp.where(owned, right, 0).astype(jnp.float32)
        slot = jnp.where(owned, node * 2 + right, -1)
        slot_hot = jnp.where(iota16 == slot, one, zero).astype(jnp.bfloat16)
        return side_sums + lax.dot_general(
            slot_hot, both.astype(jnp.bfloat16), NT, preferred_element_type=jnp.float32
        )

    side_sums = lax.fori_loop(
        0, rows // LANE_BLOCK, prepare, jnp.zeros((16, 64), jnp.float32)
    )
    x_buf[x] = jnp.concatenate([side_sums[:8], side_sums[8:]], axis=1)

    def remote(src, dst, send, recv, peer):
        return pltpu.make_async_remote_copy(
            src_ref=src,
            dst_ref=dst,
            send_sem=send,
            recv_sem=recv,
            device_id=peer,
            device_id_type=MESH,
        )

    def exchange(buf, send, recv, mine, count, peer):
        def copy(d, slot):
            return remote(buf.at[slot], buf.at[slot], send.at[d - 1], recv.at[slot], peer(d))

        def start():
            for d in range(1, count):
                copy(d, mine).start()

        def arrive():
            for d in range(1, count):
                copy(d, (mine + d) % count).wait_recv()

        def finish():
            for d in range(1, count):
                copy(d, mine).wait_send()

        return start, arrive, finish

    flags = exchange(flag_buf, flag_send, flag_recv, x, 4, x_peer)
    along_x = exchange(x_buf, x_send, x_recv, x, 4, x_peer)
    in_group = exchange(group_buf, group_send, group_recv, group, 16, group_peer)
    along_z = exchange(wide_buf, wide_send, wide_recv, wide, 4, wide_peer)
    pair_copy = remote(
        pair_buf.at[0], pair_buf.at[1], pair_send.at[0], pair_recv.at[0], z_peer2
    )
    far_copy = remote(far_flag.at[0], far_flag.at[1], far_send.at[0], far_recv.at[0], far_peer)

    def total(buf, count):
        sums = buf[0]
        for i in range(1, count):
            sums = sums + buf[i]
        return sums

    def after_x():
        along_x[1]()
        group_buf[group] = total(x_buf, 4)
        in_group[0]()

    def after_group():
        in_group[1]()
        pair_buf[0] = total(group_buf, 16)
        pair_copy.start()

    def after_pair():
        pair_copy.wait_recv()
        wide_buf[wide] = pair_buf[0] + pair_buf[1]
        along_z[0]()

    def core_copy(k):
        return remote(
            hist.at[2 * k], core_buf.at[k], core_send.at[k], core_recv.at[k], core_peer
        )

    first_y = (ya, yb)
    second_y = (yb, ya)

    def chunk_of(u):
        return u // 2 if u < 4 else 2 + u % 2

    def region(u, dest, first, count):
        high = 2 * chunk_of(u) + 1
        if u < 4:
            return high, slice(None), pl.ds(2 * dest, 2), pl.ds(32 * (u % 2) + first // 2, count // 2)
        return high, slice(None), 2 * dest + (u - 4) // 2, pl.ds(first, count)

    def part_of(u, dest, colour):
        return region(u, dest, 32 * colour, 32)

    def slots(u, early, late):
        return early.at[u] if u < 4 else late.at[u - 4]

    def y1_copy(u, colour, part):
        dest = first_y[colour] if part else yc
        return remote(
            hist.at[part_of(u, dest, colour)],
            slots(u, y1_buf, y1_late).at[colour, part],
            y1_send.at[u, colour, part],
            y1_recv.at[u, colour, part],
            at_y(first_y[colour]),
        )

    def y2_copy(u, colour):
        dest = second_y[colour]
        return remote(
            hist.at[part_of(u, dest, colour)],
            slots(u, y2_buf, y2_late).at[colour],
            y2_send.at[u, colour],
            y2_recv.at[u, colour],
            at_y(dest),
        )

    def z1_copy(u):
        return remote(
            hist.at[region(u, y, 0, 64)],
            slots(u, z1_buf, z1_late),
            z1_send.at[u],
            z1_recv.at[u],
            z_peer1,
        )

    def direct_copy(half, d):
        other = (quad + d) % 4
        return remote(
            hist.at[2 * z0 + 1, other % 2, 2 * y + other // 2, pl.ds(32 * half, 32)],
            direct_buf.at[half, d - 1],
            direct_send.at[half, d - 1],
            direct_recv.at[half, d - 1],
            at_z(other * 2 + z0),
        )

    def late_copy(nodes, high):
        other = 2 * nodes + high
        d = (other + 4 - quad) % 4
        return d, remote(
            hist.at[2 * (2 + z0) + 1, high, 2 * y + nodes],
            direct_late.at[d],
            late_send.at[nodes, high],
            late_recv.at[d],
            at_z(other * 2 + z0),
        )

    iota64 = lax.broadcasted_iota(jnp.int32, (64, rows), 0)

    def after_core(k):
        core_copy(k).wait_recv()
        hist[2 * k + 1] = hist[2 * k + 1] + core_buf[k]

    def send_y1(u):
        for part in range(2):
            for colour in range(2):
                y1_copy(u, colour, part).start()

    def add(at, incoming):
        hist[at] = hist[at] + incoming

    def after_y1(u):
        for colour in range(2):
            y1_copy(u, colour, 0).wait_recv()
            add(part_of(u, second_y[colour], colour), slots(u, y1_buf, y1_late)[colour, 0])
            y2_copy(u, colour).start()
        for colour in range(2):
            y1_copy(u, colour, 1).wait_recv()
            add(part_of(u, y, colour), slots(u, y1_buf, y1_late)[colour, 1])

    def after_y2(u):
        for colour in range(2):
            y2_copy(u, colour).wait_recv()
            add(part_of(u, y, colour), slots(u, y2_buf, y2_late)[colour])

        @pl.when(z0 != chunk_of(u) % 2)
        def _():
            z1_copy(u).start()

    def after_z1(u):
        @pl.when(z0 == chunk_of(u) % 2)
        def _():
            z1_copy(u).wait_recv()
            add(region(u, y, 0, 64), slots(u, z1_buf, z1_late)[...])
            if u < 4:
                for d in (2, 1, 3):
                    direct_copy(u % 2, d).start()
            else:
                for high in range(2):
                    d, copy = late_copy((u - 4) // 2, high)

                    @pl.when(d != 0)
                    def _():
                        copy.start()

    def step(s, carry):
        k = s // 2
        side = s % 2
        half, pair = k % 2, k // 2
        owner = side * core + (1 - side) * (1 - core)
        base = half * 8 + owner * 4 + pair * 2
        for high in range(2):
            for low in range(2):
                code = codes_ref[pl.ds(base + 16 * high + low, 1), :]
                start = (high * 2 + low) * 64
                hot[start : start + 64, :] = jnp.where(code == iota64, one, zero).astype(
                    jnp.bfloat16
                )
        out = lax.dot_general(masked[...], hot[...], NT, preferred_element_type=jnp.float32)
        for high in range(2):
            for n in range(8):
                hist[s, high, n] = out[n * 64 : (n + 1) * 64, high * 128 : (high + 1) * 128]

        @pl.when(s == 0)
        def _():
            pl.semaphore_wait(barrier, len(greeted))
            signal(vouch4, ring4)
            signal(vouch4, z_peer4)
            signal(vouch2, z_peer2)

        @pl.when(side == 0)
        def _():
            core_copy(k).start()

        @pl.when(s == 0)
        def _():
            along_x[0]()
            flags[0]()

        @pl.when((side == 0) & (k > 0))
        def _():
            after_core(k - 1)

        @pl.when(s == 2)
        def _():
            send_y1(0)
            send_y1(1)

        @pl.when(s == 3)
        def _():
            after_x()

        @pl.when(s == 4)
        def _():
            send_y1(2)

        @pl.when(s == 5)
        def _():
            after_y1(0)
            send_y1(3)

        @pl.when(s == 6)
        def _():
            after_y1(1)
            send_y1(4)

        @pl.when(s == 7)
        def _():
            after_group()

        return carry

    lax.fori_loop(0, 8, step, 0)

    for u in range(2, 8):
        after_y1(u)
        if u == 2:
            after_core(3)
        if u + 3 < 8:
            send_y1(u + 3)
        after_y2(u - 2)
        if u == 2:
            pl.semaphore_wait(vouch4, 2)
            pl.semaphore_wait(vouch2, 1)
            flags[1]()
            far_flag[0] = total(flag_buf, 4)
            far_copy.start()
        if u == 3:
            after_pair()
        if u >= 4:
            after_z1(u - 4)
    after_y2(6)
    after_z1(4)
    after_y2(7)
    after_z1(5)
    after_z1(6)
    after_z1(7)

    along_z[1]()
    sums = total(wide_buf, 4)
    sums = jnp.concatenate([sums, pltpu.roll(sums, 64, 1)], axis=0)
    sums_t = jnp.transpose(sums)[:64, :]
    leaves_t = -sums_t[:32] / (sums_t[32:] + reg_lambda)
    leaves = jnp.transpose(leaves_t)
    for n in range(8):
        leaves_ref[n] = leaves[2 * n : 2 * n + 2, :]
    far_copy.wait_recv()

    def update(i, carry):
        at = pl.ds(pl.multiple_of(i * LANE_BLOCK, LANE_BLOCK), LANE_BLOCK)
        count = far_flag[0, :, at] + far_flag[1, :, at]
        slot = nodes_ref[:, at] * 2 + jnp.where(count > 0.5, 1, 0)
        slot_hot = jnp.where(iota16 == slot, one, zero).astype(jnp.bfloat16)
        new_ref[:, at] = logits_ref[:, at] + step_size * exact_dot(leaves_t, slot_hot, NN)
        return carry

    lax.fori_loop(0, rows // LANE_BLOCK, update, 0)
    stores[0].start()
    stores[1].start()

    lane_in = lax.broadcasted_iota(jnp.int32, (128, 128), 0)
    lane_out = lax.broadcasted_iota(jnp.int32, (128, 128), 1)
    same = (lane_in // BINS) == (lane_out // BINS)
    bin_in, bin_out = lane_in % BINS, lane_out % BINS
    as_weights = lambda mask: jnp.where(mask, one, zero).astype(jnp.bfloat16)
    lower = as_weights(same & (bin_in < bin_out) & (bin_in < BINS - 1))
    every = as_weights(same)
    last = as_weights(same & (bin_in == BINS - 1))
    lane = lax.broadcasted_iota(jnp.int32, (1, 128), 1)
    for pair in range(2):
        if pair == 0:
            parts = []
            for half in range(2):
                part = hist[2 * z0 + 1, z1, 2 * y + z2, 32 * half : 32 * half + 32]
                for d in (1, 2, 3):
                    direct_copy(half, d).wait_recv()
                    part = part + direct_buf[half, d - 1]
                parts.append(part)
            owned = jnp.concatenate(parts, axis=0)
        else:
            owned = hist[2 * (2 + z0) + 1, z1, 2 * y + z2]
            for d in (1, 2, 3):
                slot = direct_late.at[d]
                remote(slot, slot, late_send.at[0, 0], late_recv.at[d], z_peer2).wait_recv()
                owned = owned + direct_late[d]
        left_base = exact_dot(owned, lower, NN)
        node_total = exact_dot(owned, every, NN)
        left_miss = left_base + exact_dot(owned, last, NN)
        parent = ratio(node_total)
        gain_left = (ratio(left_miss) + ratio(node_total - left_miss) - parent) / 64.0
        gain_right = (ratio(left_base) + ratio(node_total - left_base) - parent) / 64.0
        gain_ref[0, 2 * pair : 2 * pair + 1, :] = jnp.where(
            lane < BINS, gain_left, pltpu.roll(gain_right, BINS, 1)
        )
        gain_ref[0, 2 * pair + 1 : 2 * pair + 2, :] = jnp.where(
            lane < BINS, pltpu.roll(gain_left, BINS, 1), gain_right
        )

    stores[2].start()
    for stage in (flags, along_x, in_group, along_z):
        stage[2]()
    far_copy.wait_send()
    pair_copy.wait_send()
    for k in range(4):
        core_copy(k).wait_send()
    for u in range(8):
        for colour in range(2):
            y1_copy(u, colour, 0).wait_send()
            y1_copy(u, colour, 1).wait_send()
            y2_copy(u, colour).wait_send()
    for u in range(8):

        @pl.when(z0 != chunk_of(u) % 2)
        def _():
            z1_copy(u).wait_send()

    for half in range(2):
        for d in (1, 2, 3):
            direct_copy(half, d).wait_send()
    for nodes in range(2):
        for high in range(2):
            d, copy = late_copy(nodes, high)

            @pl.when(d != 0)
            def _():
                copy.wait_send()

    for store in stores:
        store.wait()


def move(new_ref, gain_ref, leaves_ref, new_out, gain_out, leaves_out, new_held, gain_held, leaves_held, sems):
    width = new_ref.shape[1] // 4
    parts = [(leaves_ref, leaves_held, leaves_out), (gain_ref, gain_held, gain_out)]
    for i in range(4):
        at = (slice(None), pl.ds(i * width, width))
        parts.append((new_ref.at[at], new_held.at[at], new_out.at[at]))
    loads = [pltpu.make_async_copy(a, b, sems.at[0, i]) for i, (a, b, _) in enumerate(parts)]
    stores = [pltpu.make_async_copy(b, c, sems.at[1, i]) for i, (_, b, c) in enumerate(parts)]
    for load in loads:
        load.start()
    for load, store in zip(loads, stores):
        load.wait()
        store.start()
    for store in stores:
        store.wait()


def local(logits, labels, node_ids, bin_codes, split_feature, split_bin, split_missing):
    rows = logits.shape[0]
    f32, i32 = jnp.float32, jnp.int32
    hbm = pl.BlockSpec(memory_space=pl.ANY)
    dma = pltpu.SemaphoreType.DMA
    out_shape = (
        jax.ShapeDtypeStruct((32, rows), f32),
        jax.ShapeDtypeStruct((1, 4, 128), f32),
        jax.ShapeDtypeStruct((8, 2, 32), f32),
    )
    results = pl.pallas_call(
        kernel,
        out_shape=out_shape,
        in_specs=[hbm] * 7,
        out_specs=(hbm, hbm, hbm),
        scratch_shapes=[
            pltpu.VMEM((32, rows), f32),
            pltpu.VMEM((1, 4, 128), f32),
            pltpu.VMEM((8, 2, 32), f32),
            pltpu.SMEM((8,), i32),
            pltpu.SMEM((8,), i32),
            pltpu.SMEM((8,), i32),
            pltpu.VMEM((32, rows), f32),
            pltpu.VMEM((1, rows), i32),
            pltpu.VMEM((1, rows), i32),
            pltpu.VMEM((32, rows), i32),
            pltpu.VMEM((512, rows), jnp.bfloat16),
            pltpu.VMEM((256, rows), jnp.bfloat16),
            pltpu.VMEM((8, 2, 8, 64, 128), f32),
            pltpu.VMEM((4, 2, 8, 64, 128), f32),
            pltpu.VMEM((4, 2, 2, 2, 2, 16, 128), f32),
            pltpu.VMEM((4, 2, 2, 2, 32, 128), f32),
            pltpu.VMEM((4, 2, 2, 2, 16, 128), f32),
            pltpu.VMEM((4, 2, 2, 32, 128), f32),
            pltpu.VMEM((4, 2, 2, 32, 128), f32),
            pltpu.VMEM((4, 2, 64, 128), f32),
            pltpu.VMEM((2, 3, 32, 128), f32),
            pltpu.VMEM((4, 64, 128), f32),
            pltpu.VMEM((4, 1, rows), f32),
            pltpu.VMEM((2, 1, rows), f32),
            pltpu.VMEM((4, 8, 128), f32),
            pltpu.VMEM((16, 8, 128), f32),
            pltpu.VMEM((2, 8, 128), f32),
            pltpu.VMEM((4, 8, 128), f32),
            dma((7,)),
            dma((3,)),
            dma((4,)),
            dma((4,)),
            dma((8, 2, 2)),
            dma((8, 2, 2)),
            dma((8, 2)),
            dma((8, 2)),
            dma((8,)),
            dma((8,)),
            dma((2, 3)),
            dma((2, 3)),
            dma((2, 2)),
            dma((4,)),
            dma((3,)),
            dma((4,)),
            dma((1,)),
            dma((1,)),
            dma((3,)),
            dma((4,)),
            dma((15,)),
            dma((16,)),
            dma((1,)),
            dma((1,)),
            dma((3,)),
            dma((4,)),
            pltpu.SemaphoreType.REGULAR,
            pltpu.SemaphoreType.REGULAR,
        ],
        compiler_params=pltpu.CompilerParams(
            collective_id=0, has_side_effects=True, vmem_limit_bytes=56 * 1024 * 1024
        ),
    )(
        split_feature,
        split_bin,
        split_missing,
        logits.T,
        labels.reshape(1, rows),
        node_ids.reshape(1, rows),
        bin_codes.T,
    )
    new_t, gains, leaves = pl.pallas_call(
        move,
        out_shape=out_shape,
        in_specs=[hbm] * 3,
        out_specs=(hbm, hbm, hbm),
        scratch_shapes=[
            pltpu.VMEM((32, rows), f32),
            pltpu.VMEM((1, 4, 128), f32),
            pltpu.VMEM((8, 2, 32), f32),
            dma((2, 6)),
        ],
    )(*results)
    return new_t.T, gains, leaves


def solution(mesh):
    return jax.shard_map(
        local,
        mesh=mesh,
        in_specs=(P("rows", None), P("rows"), P("rows"), P("rows", "feat"), P(), P(), P()),
        out_specs=(P("rows", None), P("rows", "feat", None), P()),
        check_vma=False,
    )
```

```python
import jax
import jax.numpy as jnp
from jax import lax
from jax.experimental import pallas as pl
from jax.experimental.pallas import tpu as pltpu
from jax.sharding import PartitionSpec as P

BINS = 64
MESH = pl.DeviceIdType.MESH
reg_lambda = 1.0
step_size = 0.3
LANE_BLOCK = 512
NT = (((1,), (1,)), ((), ()))
NN = (((1,), (0,)), ((), ()))


def split3(x):
    hi = x.astype(jnp.bfloat16)
    rest = x - hi.astype(jnp.float32)
    mid = rest.astype(jnp.bfloat16)
    low = (rest - mid.astype(jnp.float32)).astype(jnp.bfloat16)
    return hi, mid, low


def exact_dot(x, weights, dims):
    hi, mid, low = split3(x)
    dot = lambda part: lax.dot_general(part, weights, dims, preferred_element_type=jnp.float32)
    return dot(hi) + (dot(mid) + dot(low))


def ratio(sums):
    grad_part = sums[:32]
    hess_part = sums[32:]
    return jnp.sum(grad_part * grad_part / (hess_part + reg_lambda), axis=0, keepdims=True)


def kernel(
    feature_hbm,
    bin_hbm,
    missing_hbm,
    logits_hbm,
    labels_hbm,
    nodes_hbm,
    codes_hbm,
    new_hbm,
    gain_hbm,
    leaves_hbm,
    new_ref,
    gain_ref,
    leaves_ref,
    feature_ref,
    bin_ref,
    missing_ref,
    logits_ref,
    labels_ref,
    nodes_ref,
    codes_ref,
    masked,
    hot,
    hist,
    core_buf,
    y1_buf,
    y2_buf,
    z1_buf,
    direct_buf,
    flag_buf,
    far_flag,
    x_buf,
    group_buf,
    pair_buf,
    wide_buf,
    load_sem,
    store_sem,
    core_send,
    core_recv,
    y1_send,
    y1_recv,
    y2_send,
    y2_recv,
    z1_send,
    z1_recv,
    direct_send,
    direct_recv,
    flag_send,
    flag_recv,
    far_send,
    far_recv,
    x_send,
    x_recv,
    group_send,
    group_recv,
    pair_send,
    pair_recv,
    wide_send,
    wide_recv,
    vouch4,
    vouch2,
):
    rows = logits_ref.shape[1]
    row = lax.axis_index("rows")
    feat = lax.axis_index("feat")
    core = row % 2
    z = (row // 2) % 8
    y = row // 16
    x, z_hi = feat // 2, feat % 2
    z0, z1, z2 = z % 2, (z // 2) % 2, z // 4
    quad = z // 2
    group = (y * 2 + core) * 2 + z0
    wide = z_hi * 2 + z2
    ya = y + 1 - 2 * (y % 2)
    yb = 3 - y
    yc = 3 - ya

    loads = [
        pltpu.make_async_copy(src, dst, load_sem.at[i])
        for i, (src, dst) in enumerate(
            (
                (logits_hbm, logits_ref),
                (labels_hbm, labels_ref),
                (nodes_hbm, nodes_ref),
                (codes_hbm, codes_ref),
                (feature_hbm, feature_ref),
                (bin_hbm, bin_ref),
                (missing_hbm, missing_ref),
            )
        )
    ]
    for load in loads:
        load.start()
    stores = [
        pltpu.make_async_copy(src, dst, store_sem.at[i])
        for i, (src, dst) in enumerate(
            ((new_ref, new_hbm), (leaves_ref, leaves_hbm), (gain_ref, gain_hbm))
        )
    ]

    def at_y(other):
        return (other * 16 + z * 2 + core, feat)

    def at_z(other):
        return (y * 16 + other * 2 + core, feat)

    core_peer = (row + 1 - 2 * core, feat)
    z_peer1 = at_z(z + 1 - 2 * z0)
    z_peer2 = at_z(z + 2 - 4 * z1)
    z_peer4 = at_z(z + 4 - 8 * z2)
    far_peer = (row, x * 2 + 1 - z_hi)
    ring4 = (y * 16 + ((z + 4) % 8) * 2 + core, x * 2 + 1 - z_hi)

    def x_peer(d):
        return (row, ((x + d) % 4) * 2 + z_hi)

    def group_peer(d):
        other = (group + d) % 16
        return ((other // 4) * 16 + (z - z0 + other % 2) * 2 + (other // 2) % 2, feat)

    def wide_peer(d):
        other = (wide + d) % 4
        return (y * 16 + (z % 4 + 4 * (other % 2)) * 2 + core, x * 2 + other // 2)

    def signal(sem, peer):
        pl.semaphore_signal(sem, inc=1, device_id=peer, device_id_type=MESH)

    barrier = pltpu.get_barrier_semaphore()
    greeted = [ring4, z_peer4, z_peer2]
    greeted += [x_peer(d) for d in range(1, 4)] + [group_peer(d) for d in range(1, 16)]
    for peer in greeted:
        signal(barrier, peer)

    iota16 = lax.broadcasted_iota(jnp.int32, (16, LANE_BLOCK), 0)
    iota32 = lax.broadcasted_iota(jnp.int32, (32, LANE_BLOCK), 0)
    one, zero = jnp.float32(1.0), jnp.float32(0.0)

    for load in loads:
        load.wait()

    def prepare(i, side_sums):
        at = pl.ds(pl.multiple_of(i * LANE_BLOCK, LANE_BLOCK), LANE_BLOCK)
        expo = jnp.exp(logits_ref[:, at])
        prob = expo / jnp.sum(expo, axis=0, keepdims=True)
        target = jnp.where(iota32 == labels_ref[:, at], one, zero)
        grad = (prob - target).astype(jnp.bfloat16).astype(jnp.float32)
        hess = (prob * (1.0 - prob)).astype(jnp.bfloat16).astype(jnp.float32)
        both = jnp.concatenate([grad, hess], axis=0)
        node = nodes_ref[:, at]
        row_feature = jnp.zeros_like(node)
        row_bin = jnp.zeros_like(node)
        row_missing = jnp.zeros_like(node)
        for n in range(8):
            here = node == n
            masked[n * 64 : (n + 1) * 64, at] = jnp.where(here, both, zero).astype(jnp.bfloat16)
            row_feature = jnp.where(here, feature_ref[n], row_feature)
            row_bin = jnp.where(here, bin_ref[n], row_bin)
            row_missing = jnp.where(here, missing_ref[n], row_missing)
        column = row_feature - feat * 32
        owned = (column >= 0) & (column < 32)
        code = jnp.sum(
            jnp.where(iota32 == column, codes_ref[:, at].astype(jnp.float32), zero),
            axis=0,
            keepdims=True,
        ).astype(jnp.int32)
        left = (code < row_bin) | ((code == BINS - 1) & (row_missing == 1))
        right = jnp.where(left, 0, 1)
        flag_buf[x, :, at] = jnp.where(owned, right, 0).astype(jnp.float32)
        slot = jnp.where(owned, node * 2 + right, -1)
        slot_hot = jnp.where(iota16 == slot, one, zero).astype(jnp.bfloat16)
        return side_sums + lax.dot_general(
            slot_hot, both.astype(jnp.bfloat16), NT, preferred_element_type=jnp.float32
        )

    side_sums = lax.fori_loop(
        0, rows // LANE_BLOCK, prepare, jnp.zeros((16, 64), jnp.float32)
    )
    x_buf[x] = jnp.concatenate([side_sums[:8], side_sums[8:]], axis=1)

    def remote(src, dst, send, recv, peer):
        return pltpu.make_async_remote_copy(
            src_ref=src,
            dst_ref=dst,
            send_sem=send,
            recv_sem=recv,
            device_id=peer,
            device_id_type=MESH,
        )

    def exchange(buf, send, recv, mine, count, peer):
        def copy(d, slot):
            return remote(buf.at[slot], buf.at[slot], send.at[d - 1], recv.at[slot], peer(d))

        def start():
            for d in range(1, count):
                copy(d, mine).start()

        def arrive():
            for d in range(1, count):
                copy(d, (mine + d) % count).wait_recv()

        def finish():
            for d in range(1, count):
                copy(d, mine).wait_send()

        return start, arrive, finish

    flags = exchange(flag_buf, flag_send, flag_recv, x, 4, x_peer)
    along_x = exchange(x_buf, x_send, x_recv, x, 4, x_peer)
    in_group = exchange(group_buf, group_send, group_recv, group, 16, group_peer)
    along_z = exchange(wide_buf, wide_send, wide_recv, wide, 4, wide_peer)
    pair_copy = remote(
        pair_buf.at[0], pair_buf.at[1], pair_send.at[0], pair_recv.at[0], z_peer2
    )
    far_copy = remote(far_flag.at[0], far_flag.at[1], far_send.at[0], far_recv.at[0], far_peer)

    def total(buf, count):
        sums = buf[0]
        for i in range(1, count):
            sums = sums + buf[i]
        return sums

    def after_x():
        along_x[1]()
        group_buf[group] = total(x_buf, 4)
        in_group[0]()

    def after_group():
        in_group[1]()
        pair_buf[0] = total(group_buf, 16)
        pair_copy.start()

    def after_pair():
        pair_copy.wait_recv()
        wide_buf[wide] = pair_buf[0] + pair_buf[1]
        along_z[0]()

    def core_copy(k):
        return remote(
            hist.at[2 * k], core_buf.at[k], core_send.at[k], core_recv.at[k], core_peer
        )

    first_y = (ya, yb)
    second_y = (yb, ya)

    chunks = (0, 0, 1, 2, 3, 1, 2, 3)
    parities = (0, 1, 0, 0, 0, 1, 1, 1)

    def chunk_of(u):
        return chunks[u]

    def region(u, dest, first, count):
        return 2 * chunks[u] + 1, slice(None), 2 * dest + parities[u], pl.ds(first, count)

    def part_of(u, dest, colour):
        return region(u, dest, 32 * colour, 32)

    def y1_copy(u, colour, part):
        dest = first_y[colour] if part else yc
        return remote(
            hist.at[part_of(u, dest, colour)],
            y1_buf.at[u].at[colour, part],
            y1_send.at[u, colour, part],
            y1_recv.at[u, colour, part],
            at_y(first_y[colour]),
        )

    def y2_copy(u, colour):
        dest = second_y[colour]
        return remote(
            hist.at[part_of(u, dest, colour)],
            y2_buf.at[u].at[colour],
            y2_send.at[u, colour],
            y2_recv.at[u, colour],
            at_y(dest),
        )

    def z1_copy(u):
        return remote(
            hist.at[region(u, y, 0, 64)],
            z1_buf.at[u],
            z1_send.at[u],
            z1_recv.at[u],
            z_peer1,
        )

    def direct_copy(pair, nodes, high):
        other = 2 * nodes + high
        d = (other + 4 - quad) % 4
        return d, remote(
            hist.at[4 * pair + 2 * z0 + 1, high, 2 * y + nodes],
            direct_buf.at[pair, d],
            direct_send.at[pair, nodes, high],
            direct_recv.at[pair, d],
            at_z(other * 2 + z0),
        )

    iota64 = lax.broadcasted_iota(jnp.int32, (64, rows), 0)

    def after_core(k):
        core_copy(k).wait_recv()
        hist[2 * k + 1] = hist[2 * k + 1] + core_buf[k]

    def send_y1(u):
        for part in range(2):
            for colour in range(2):
                y1_copy(u, colour, part).start()

    def add(at, incoming):
        hist[at] = hist[at] + incoming

    def after_y1(u):
        for colour in range(2):
            y1_copy(u, colour, 0).wait_recv()
            add(part_of(u, second_y[colour], colour), y1_buf[u, colour, 0])
            y2_copy(u, colour).start()

    def after_y2(u):
        for colour in range(2):
            y1_copy(u, colour, 1).wait_recv()
            y2_copy(u, colour).wait_recv()
            add(
                part_of(u, y, colour),
                y1_buf[u, colour, 1] + y2_buf[u, colour],
            )

        @pl.when(z0 != chunk_of(u) % 2)
        def _():
            z1_copy(u).start()

    def after_z1(u):
        @pl.when(z0 == chunk_of(u) % 2)
        def _():
            z1_copy(u).wait_recv()
            add(region(u, y, 0, 64), z1_buf[u])
            for high in range(2):
                d, copy = direct_copy(chunks[u] // 2, parities[u], high)

                @pl.when(d != 0)
                def _():
                    copy.start()

    def step(s, carry):
        k = s // 2
        side = s % 2
        half, pair = k % 2, k // 2
        owner = side * core + (1 - side) * (1 - core)
        base = half * 8 + owner * 4 + pair * 2
        for high in range(2):
            for low in range(2):
                code = codes_ref[pl.ds(base + 16 * high + low, 1), :]
                start = (high * 2 + low) * 64
                hot[start : start + 64, :] = jnp.where(code == iota64, one, zero).astype(
                    jnp.bfloat16
                )
        out = lax.dot_general(masked[...], hot[...], NT, preferred_element_type=jnp.float32)
        for high in range(2):
            for n in range(8):
                hist[s, high, n] = out[n * 64 : (n + 1) * 64, high * 128 : (high + 1) * 128]

        @pl.when(s == 0)
        def _():
            pl.semaphore_wait(barrier, len(greeted))
            signal(vouch4, ring4)
            signal(vouch4, z_peer4)
            signal(vouch2, z_peer2)

        @pl.when(side == 0)
        def _():
            core_copy(k).start()

        @pl.when(s == 0)
        def _():
            along_x[0]()
            flags[0]()

        @pl.when((side == 0) & (k > 0))
        def _():
            after_core(k - 1)

        @pl.when(s == 2)
        def _():
            send_y1(0)
            send_y1(1)

        @pl.when(s == 3)
        def _():
            after_x()

        @pl.when(s == 4)
        def _():
            send_y1(2)

        @pl.when(s == 5)
        def _():
            after_y1(0)

        @pl.when(s == 6)
        def _():
            send_y1(3)
            after_y1(1)

        @pl.when(s == 7)
        def _():
            after_group()

        return carry

    lax.fori_loop(0, 8, step, 0)

    after_core(3)
    send_y1(4)
    for u in range(2, 8):
        after_y1(u)
        if u + 3 < 8:
            send_y1(u + 3)
        after_y2(u - 2)
        if u == 2:
            pl.semaphore_wait(vouch4, 2)
            pl.semaphore_wait(vouch2, 1)
            flags[1]()
            far_flag[0] = total(flag_buf, 4)
            far_copy.start()
        if u == 3:
            after_pair()
        if u >= 4:
            after_z1(u - 4)
    after_y2(6)
    after_z1(4)
    after_y2(7)
    after_z1(5)
    after_z1(6)
    after_z1(7)

    along_z[1]()
    sums = total(wide_buf, 4)
    sums = jnp.concatenate([sums, pltpu.roll(sums, 64, 1)], axis=0)
    sums_t = jnp.transpose(sums)[:64, :]
    leaves_t = -sums_t[:32] / (sums_t[32:] + reg_lambda)
    leaves = jnp.transpose(leaves_t)
    for n in range(8):
        leaves_ref[n] = leaves[2 * n : 2 * n + 2, :]
    far_copy.wait_recv()

    def update(i, carry):
        at = pl.ds(pl.multiple_of(i * LANE_BLOCK, LANE_BLOCK), LANE_BLOCK)
        count = far_flag[0, :, at] + far_flag[1, :, at]
        slot = nodes_ref[:, at] * 2 + jnp.where(count > 0.5, 1, 0)
        slot_hot = jnp.where(iota16 == slot, one, zero).astype(jnp.bfloat16)
        new_ref[:, at] = logits_ref[:, at] + step_size * exact_dot(leaves_t, slot_hot, NN)
        return carry

    lax.fori_loop(0, rows // LANE_BLOCK, update, 0)
    stores[0].start()
    stores[1].start()

    lane_in = lax.broadcasted_iota(jnp.int32, (128, 128), 0)
    lane_out = lax.broadcasted_iota(jnp.int32, (128, 128), 1)
    same = (lane_in // BINS) == (lane_out // BINS)
    bin_in, bin_out = lane_in % BINS, lane_out % BINS
    as_weights = lambda mask: jnp.where(mask, one, zero).astype(jnp.bfloat16)
    lower = as_weights(same & (bin_in < bin_out) & (bin_in < BINS - 1))
    every = as_weights(same)
    last = as_weights(same & (bin_in == BINS - 1))
    lane = lax.broadcasted_iota(jnp.int32, (1, 128), 1)
    for pair in range(2):
        owned = hist[4 * pair + 2 * z0 + 1, z1, 2 * y + z2]
        for d in (1, 2, 3):
            slot = direct_buf.at[pair, d]
            remote(slot, slot, direct_send.at[0, 0, 0], direct_recv.at[pair, d], z_peer2).wait_recv()
            owned = owned + direct_buf[pair, d]
        left_base = exact_dot(owned, lower, NN)
        node_total = exact_dot(owned, every, NN)
        left_miss = left_base + exact_dot(owned, last, NN)
        parent = ratio(node_total)
        gain_left = (ratio(left_miss) + ratio(node_total - left_miss) - parent) / 64.0
        gain_right = (ratio(left_base) + ratio(node_total - left_base) - parent) / 64.0
        gain_ref[0, 2 * pair : 2 * pair + 1, :] = jnp.where(
            lane < BINS, gain_left, pltpu.roll(gain_right, BINS, 1)
        )
        gain_ref[0, 2 * pair + 1 : 2 * pair + 2, :] = jnp.where(
            lane < BINS, pltpu.roll(gain_left, BINS, 1), gain_right
        )

    stores[2].start()
    for stage in (flags, along_x, in_group, along_z):
        stage[2]()
    far_copy.wait_send()
    pair_copy.wait_send()
    for k in range(4):
        core_copy(k).wait_send()
    for u in range(8):
        for colour in range(2):
            y1_copy(u, colour, 0).wait_send()
            y1_copy(u, colour, 1).wait_send()
            y2_copy(u, colour).wait_send()
    for u in range(8):

        @pl.when(z0 != chunk_of(u) % 2)
        def _():
            z1_copy(u).wait_send()

    for pair in range(2):
        for nodes in range(2):
            for high in range(2):
                d, copy = direct_copy(pair, nodes, high)

                @pl.when(d != 0)
                def _():
                    copy.wait_send()

    for store in stores:
        store.wait()


def move(new_ref, gain_ref, leaves_ref, new_out, gain_out, leaves_out, new_held, gain_held, leaves_held, sems):
    width = new_ref.shape[1] // 4
    parts = [(leaves_ref, leaves_held, leaves_out), (gain_ref, gain_held, gain_out)]
    for i in range(4):
        at = (slice(None), pl.ds(i * width, width))
        parts.append((new_ref.at[at], new_held.at[at], new_out.at[at]))
    loads = [pltpu.make_async_copy(a, b, sems.at[0, i]) for i, (a, b, _) in enumerate(parts)]
    stores = [pltpu.make_async_copy(b, c, sems.at[1, i]) for i, (_, b, c) in enumerate(parts)]
    for load in loads:
        load.start()
    for load, store in zip(loads, stores):
        load.wait()
        store.start()
    for store in stores:
        store.wait()


def local(logits, labels, node_ids, bin_codes, split_feature, split_bin, split_missing):
    rows = logits.shape[0]
    f32, i32 = jnp.float32, jnp.int32
    hbm = pl.BlockSpec(memory_space=pl.ANY)
    dma = pltpu.SemaphoreType.DMA
    out_shape = (
        jax.ShapeDtypeStruct((32, rows), f32),
        jax.ShapeDtypeStruct((1, 4, 128), f32),
        jax.ShapeDtypeStruct((8, 2, 32), f32),
    )
    results = pl.pallas_call(
        kernel,
        out_shape=out_shape,
        in_specs=[hbm] * 7,
        out_specs=(hbm, hbm, hbm),
        scratch_shapes=[
            pltpu.VMEM((32, rows), f32),
            pltpu.VMEM((1, 4, 128), f32),
            pltpu.VMEM((8, 2, 32), f32),
            pltpu.SMEM((8,), i32),
            pltpu.SMEM((8,), i32),
            pltpu.SMEM((8,), i32),
            pltpu.VMEM((32, rows), f32),
            pltpu.VMEM((1, rows), i32),
            pltpu.VMEM((1, rows), i32),
            pltpu.VMEM((32, rows), i32),
            pltpu.VMEM((512, rows), jnp.bfloat16),
            pltpu.VMEM((256, rows), jnp.bfloat16),
            pltpu.VMEM((8, 2, 8, 64, 128), f32),
            pltpu.VMEM((4, 2, 8, 64, 128), f32),
            pltpu.VMEM((8, 2, 2, 2, 32, 128), f32),
            pltpu.VMEM((8, 2, 2, 32, 128), f32),
            pltpu.VMEM((8, 2, 64, 128), f32),
            pltpu.VMEM((2, 4, 64, 128), f32),
            pltpu.VMEM((4, 1, rows), f32),
            pltpu.VMEM((2, 1, rows), f32),
            pltpu.VMEM((4, 8, 128), f32),
            pltpu.VMEM((16, 8, 128), f32),
            pltpu.VMEM((2, 8, 128), f32),
            pltpu.VMEM((4, 8, 128), f32),
            dma((7,)),
            dma((3,)),
            dma((4,)),
            dma((4,)),
            dma((8, 2, 2)),
            dma((8, 2, 2)),
            dma((8, 2)),
            dma((8, 2)),
            dma((8,)),
            dma((8,)),
            dma((2, 2, 2)),
            dma((2, 4)),
            dma((3,)),
            dma((4,)),
            dma((1,)),
            dma((1,)),
            dma((3,)),
            dma((4,)),
            dma((15,)),
            dma((16,)),
            dma((1,)),
            dma((1,)),
            dma((3,)),
            dma((4,)),
            pltpu.SemaphoreType.REGULAR,
            pltpu.SemaphoreType.REGULAR,
        ],
        compiler_params=pltpu.CompilerParams(
            collective_id=0, has_side_effects=True, vmem_limit_bytes=56 * 1024 * 1024
        ),
    )(
        split_feature,
        split_bin,
        split_missing,
        logits.T,
        labels.reshape(1, rows),
        node_ids.reshape(1, rows),
        bin_codes.T,
    )
    new_t, gains, leaves = pl.pallas_call(
        move,
        out_shape=out_shape,
        in_specs=[hbm] * 3,
        out_specs=(hbm, hbm, hbm),
        scratch_shapes=[
            pltpu.VMEM((32, rows), f32),
            pltpu.VMEM((1, 4, 128), f32),
            pltpu.VMEM((8, 2, 32), f32),
            dma((2, 6)),
        ],
    )(*results)
    return new_t.T, gains, leaves


def solution(mesh):
    return jax.shard_map(
        local,
        mesh=mesh,
        in_specs=(P("rows", None), P("rows"), P("rows"), P("rows", "feat"), P(), P(), P()),
        out_specs=(P("rows", None), P("rows", "feat", None), P()),
        check_vma=False,
    )
```

```python
import jax
import jax.numpy as jnp
from jax import lax
from jax.experimental import pallas as pl
from jax.experimental.pallas import tpu as pltpu
from jax.sharding import PartitionSpec as P

BINS = 64
MESH = pl.DeviceIdType.MESH
reg_lambda = 1.0
step_size = 0.3
LANE_BLOCK = 512
NT = (((1,), (1,)), ((), ()))
NN = (((1,), (0,)), ((), ()))


def split3(x):
    hi = x.astype(jnp.bfloat16)
    rest = x - hi.astype(jnp.float32)
    mid = rest.astype(jnp.bfloat16)
    low = (rest - mid.astype(jnp.float32)).astype(jnp.bfloat16)
    return hi, mid, low


def exact_dot(x, weights, dims):
    hi, mid, low = split3(x)
    dot = lambda part: lax.dot_general(part, weights, dims, preferred_element_type=jnp.float32)
    return dot(hi) + (dot(mid) + dot(low))


def ratio(sums):
    grad_part = sums[:32]
    hess_part = sums[32:]
    return jnp.sum(grad_part * grad_part / (hess_part + reg_lambda), axis=0, keepdims=True)


def kernel(
    feature_hbm,
    bin_hbm,
    missing_hbm,
    logits_hbm,
    labels_hbm,
    nodes_hbm,
    codes_hbm,
    new_hbm,
    gain_hbm,
    leaves_hbm,
    new_ref,
    gain_ref,
    leaves_ref,
    feature_ref,
    bin_ref,
    missing_ref,
    logits_ref,
    labels_ref,
    nodes_ref,
    codes_ref,
    masked,
    hot,
    hist,
    core_buf,
    y1_buf,
    y2_buf,
    z1_buf,
    direct_buf,
    flag_buf,
    far_flag,
    x_buf,
    group_buf,
    pair_buf,
    wide_buf,
    load_sem,
    store_sem,
    core_send,
    core_recv,
    y1_send,
    y1_recv,
    y2_send,
    y2_recv,
    z1_send,
    z1_recv,
    direct_send,
    direct_recv,
    flag_send,
    flag_recv,
    far_send,
    far_recv,
    x_send,
    x_recv,
    group_send,
    group_recv,
    pair_send,
    pair_recv,
    wide_send,
    wide_recv,
    vouch4,
    vouch2,
):
    rows = logits_ref.shape[1]
    row = lax.axis_index("rows")
    feat = lax.axis_index("feat")
    core = row % 2
    z = (row // 2) % 8
    y = row // 16
    x, z_hi = feat // 2, feat % 2
    z0, z1, z2 = z % 2, (z // 2) % 2, z // 4
    quad = z // 2
    group = (y * 2 + core) * 2 + z0
    wide = z_hi * 2 + z2
    ya = y + 1 - 2 * (y % 2)
    yb = 3 - y
    yc = 3 - ya

    loads = [
        pltpu.make_async_copy(src, dst, load_sem.at[i])
        for i, (src, dst) in enumerate(
            (
                (logits_hbm, logits_ref),
                (labels_hbm, labels_ref),
                (nodes_hbm, nodes_ref),
                (codes_hbm, codes_ref),
                (feature_hbm, feature_ref),
                (bin_hbm, bin_ref),
                (missing_hbm, missing_ref),
            )
        )
    ]
    for load in loads:
        load.start()
    stores = [
        pltpu.make_async_copy(src, dst, store_sem.at[i])
        for i, (src, dst) in enumerate(
            ((new_ref, new_hbm), (leaves_ref, leaves_hbm), (gain_ref, gain_hbm))
        )
    ]

    def at_y(other):
        return (other * 16 + z * 2 + core, feat)

    def at_z(other):
        return (y * 16 + other * 2 + core, feat)

    core_peer = (row + 1 - 2 * core, feat)
    z_peer1 = at_z(z + 1 - 2 * z0)
    z_peer2 = at_z(z + 2 - 4 * z1)
    z_peer4 = at_z(z + 4 - 8 * z2)
    far_peer = (row, x * 2 + 1 - z_hi)
    ring4 = (y * 16 + ((z + 4) % 8) * 2 + core, x * 2 + 1 - z_hi)

    def x_peer(d):
        return (row, ((x + d) % 4) * 2 + z_hi)

    def group_peer(d):
        other = (group + d) % 16
        return ((other // 4) * 16 + (z - z0 + other % 2) * 2 + (other // 2) % 2, feat)

    def wide_peer(d):
        other = (wide + d) % 4
        return (y * 16 + (z % 4 + 4 * (other % 2)) * 2 + core, x * 2 + other // 2)

    def signal(sem, peer):
        pl.semaphore_signal(sem, inc=1, device_id=peer, device_id_type=MESH)

    barrier = pltpu.get_barrier_semaphore()
    greeted = [ring4, z_peer4, z_peer2]
    greeted += [x_peer(d) for d in range(1, 4)] + [group_peer(d) for d in range(1, 16)]
    for peer in greeted:
        signal(barrier, peer)

    iota16 = lax.broadcasted_iota(jnp.int32, (16, LANE_BLOCK), 0)
    iota32 = lax.broadcasted_iota(jnp.int32, (32, LANE_BLOCK), 0)
    one, zero = jnp.float32(1.0), jnp.float32(0.0)

    for load in loads:
        load.wait()

    def prepare(i, side_sums):
        at = pl.ds(pl.multiple_of(i * LANE_BLOCK, LANE_BLOCK), LANE_BLOCK)
        expo = jnp.exp(logits_ref[:, at])
        prob = expo / jnp.sum(expo, axis=0, keepdims=True)
        target = jnp.where(iota32 == labels_ref[:, at], one, zero)
        grad = (prob - target).astype(jnp.bfloat16).astype(jnp.float32)
        hess = (prob * (1.0 - prob)).astype(jnp.bfloat16).astype(jnp.float32)
        both = jnp.concatenate([grad, hess], axis=0)
        node = nodes_ref[:, at]
        row_feature = jnp.zeros_like(node)
        row_bin = jnp.zeros_like(node)
        row_missing = jnp.zeros_like(node)
        for n in range(8):
            here = node == n
            masked[n * 64 : (n + 1) * 64, at] = jnp.where(here, both, zero).astype(jnp.bfloat16)
            row_feature = jnp.where(here, feature_ref[n], row_feature)
            row_bin = jnp.where(here, bin_ref[n], row_bin)
            row_missing = jnp.where(here, missing_ref[n], row_missing)
        column = row_feature - feat * 32
        owned = (column >= 0) & (column < 32)
        code = jnp.sum(
            jnp.where(iota32 == column, codes_ref[:, at].astype(jnp.float32), zero),
            axis=0,
            keepdims=True,
        ).astype(jnp.int32)
        left = (code < row_bin) | ((code == BINS - 1) & (row_missing == 1))
        right = jnp.where(left, 0, 1)
        flag_buf[x, :, at] = jnp.where(owned, right, 0).astype(jnp.float32)
        slot = jnp.where(owned, node * 2 + right, -1)
        slot_hot = jnp.where(iota16 == slot, one, zero).astype(jnp.bfloat16)
        return side_sums + lax.dot_general(
            slot_hot, both.astype(jnp.bfloat16), NT, preferred_element_type=jnp.float32
        )

    side_sums = lax.fori_loop(
        0, rows // LANE_BLOCK, prepare, jnp.zeros((16, 64), jnp.float32)
    )
    x_buf[x] = jnp.concatenate([side_sums[:8], side_sums[8:]], axis=1)

    def remote(src, dst, send, recv, peer):
        return pltpu.make_async_remote_copy(
            src_ref=src,
            dst_ref=dst,
            send_sem=send,
            recv_sem=recv,
            device_id=peer,
            device_id_type=MESH,
        )

    def exchange(buf, send, recv, mine, count, peer):
        def copy(d, slot):
            return remote(buf.at[slot], buf.at[slot], send.at[d - 1], recv.at[slot], peer(d))

        def start():
            for d in range(1, count):
                copy(d, mine).start()

        def arrive():
            for d in range(1, count):
                copy(d, (mine + d) % count).wait_recv()

        def finish():
            for d in range(1, count):
                copy(d, mine).wait_send()

        return start, arrive, finish

    flags = exchange(flag_buf, flag_send, flag_recv, x, 4, x_peer)
    along_x = exchange(x_buf, x_send, x_recv, x, 4, x_peer)
    in_group = exchange(group_buf, group_send, group_recv, group, 16, group_peer)
    along_z = exchange(wide_buf, wide_send, wide_recv, wide, 4, wide_peer)
    pair_copy = remote(
        pair_buf.at[0], pair_buf.at[1], pair_send.at[0], pair_recv.at[0], z_peer2
    )
    far_copy = remote(far_flag.at[0], far_flag.at[1], far_send.at[0], far_recv.at[0], far_peer)

    def total(buf, count):
        sums = buf[0]
        for i in range(1, count):
            sums = sums + buf[i]
        return sums

    def after_x():
        along_x[1]()
        group_buf[group] = total(x_buf, 4)
        in_group[0]()

    def after_group():
        in_group[1]()
        pair_buf[0] = total(group_buf, 16)
        pair_copy.start()

    def after_pair():
        pair_copy.wait_recv()
        wide_buf[wide] = pair_buf[0] + pair_buf[1]
        along_z[0]()

    def core_copy(k):
        return remote(
            hist.at[2 * k], core_buf.at[k], core_send.at[k], core_recv.at[k], core_peer
        )

    first_y = (ya, yb)
    second_y = (yb, ya)

    chunks = (0, 0, 1, 2, 3, 1, 2, 3)
    parities = (0, 1, 0, 0, 0, 1, 1, 1)

    def chunk_of(u):
        return chunks[u]

    def region(u, dest, first, count):
        return 2 * chunks[u] + 1, slice(None), 2 * dest + parities[u], pl.ds(first, count)

    def part_of(u, dest, colour):
        return region(u, dest, 32 * colour, 32)

    def y1_copy(u, colour, part):
        dest = first_y[colour] if part else yc
        return remote(
            hist.at[part_of(u, dest, colour)],
            y1_buf.at[u].at[colour, part],
            y1_send.at[u, colour, part],
            y1_recv.at[u, colour, part],
            at_y(first_y[colour]),
        )

    def y2_copy(u, colour):
        dest = second_y[colour]
        return remote(
            hist.at[part_of(u, dest, colour)],
            y2_buf.at[u].at[colour],
            y2_send.at[u, colour],
            y2_recv.at[u, colour],
            at_y(dest),
        )

    def z1_copy(u):
        return remote(
            hist.at[region(u, y, 0, 64)],
            z1_buf.at[u],
            z1_send.at[u],
            z1_recv.at[u],
            z_peer1,
        )

    def direct_copy(pair, nodes, high):
        other = 2 * nodes + high
        d = (other + 4 - quad) % 4
        return d, remote(
            hist.at[4 * pair + 2 * z0 + 1, high, 2 * y + nodes],
            direct_buf.at[pair, d],
            direct_send.at[pair, nodes, high],
            direct_recv.at[pair, d],
            at_z(other * 2 + z0),
        )

    iota64 = lax.broadcasted_iota(jnp.int32, (64, rows), 0)

    def after_core(k):
        core_copy(k).wait_recv()
        hist[2 * k + 1] = hist[2 * k + 1] + core_buf[k]

    def send_y1(u):
        for part in range(2):
            for colour in range(2):
                y1_copy(u, colour, part).start()

    def add(at, incoming):
        hist[at] = hist[at] + incoming

    def after_y1(u):
        for colour in range(2):
            y1_copy(u, colour, 0).wait_recv()
            add(part_of(u, second_y[colour], colour), y1_buf[u, colour, 0])
            y2_copy(u, colour).start()

    def after_y2(u):
        for colour in range(2):
            y1_copy(u, colour, 1).wait_recv()
            y2_copy(u, colour).wait_recv()
            add(
                part_of(u, y, colour),
                y1_buf[u, colour, 1] + y2_buf[u, colour],
            )

        @pl.when(z0 != chunk_of(u) % 2)
        def _():
            z1_copy(u).start()

    def after_z1(u):
        @pl.when(z0 == chunk_of(u) % 2)
        def _():
            z1_copy(u).wait_recv()
            add(region(u, y, 0, 64), z1_buf[u])
            for high in range(2):
                d, copy = direct_copy(chunks[u] // 2, parities[u], high)

                @pl.when(d != 0)
                def _():
                    copy.start()

    def step(s, carry):
        k = s // 2
        side = s % 2
        half, pair = k % 2, k // 2
        owner = side * core + (1 - side) * (1 - core)
        base = half * 8 + owner * 4 + pair * 2
        for high in range(2):
            for low in range(2):
                code = codes_ref[pl.ds(base + 16 * high + low, 1), :]
                start = (high * 2 + low) * 64
                hot[start : start + 64, :] = jnp.where(code == iota64, one, zero).astype(
                    jnp.bfloat16
                )
        out = lax.dot_general(masked[...], hot[...], NT, preferred_element_type=jnp.float32)
        for high in range(2):
            for n in range(8):
                hist[s, high, n] = out[n * 64 : (n + 1) * 64, high * 128 : (high + 1) * 128]

        @pl.when(s == 0)
        def _():
            pl.semaphore_wait(barrier, len(greeted))
            signal(vouch4, ring4)
            signal(vouch4, z_peer4)
            signal(vouch2, z_peer2)

        @pl.when(side == 0)
        def _():
            core_copy(k).start()

        @pl.when(s == 0)
        def _():
            along_x[0]()
            flags[0]()

        @pl.when((side == 0) & (k > 0))
        def _():
            after_core(k - 1)

        @pl.when(s == 2)
        def _():
            send_y1(0)
            send_y1(1)

        @pl.when(s == 3)
        def _():
            after_x()

        @pl.when(s == 4)
        def _():
            send_y1(2)

        @pl.when(s == 5)
        def _():
            after_y1(0)

        @pl.when(s == 6)
        def _():
            send_y1(3)
            after_y1(1)

        @pl.when(s == 7)
        def _():
            after_group()

        return carry

    lax.fori_loop(0, 8, step, 0)

    after_core(3)
    send_y1(4)
    for u in range(2, 8):
        after_y1(u)
        if u + 3 < 8:
            send_y1(u + 3)
        if u >= 4:
            after_z1(u - 4)
        after_y2(u - 2)
        if u == 2:
            pl.semaphore_wait(vouch4, 2)
            pl.semaphore_wait(vouch2, 1)
            flags[1]()
            far_flag[0] = total(flag_buf, 4)
            far_copy.start()
        if u == 3:
            after_pair()
    after_y2(6)
    after_z1(4)
    after_y2(7)
    after_z1(5)
    after_z1(6)
    after_z1(7)

    along_z[1]()
    sums = total(wide_buf, 4)
    sums = jnp.concatenate([sums, pltpu.roll(sums, 64, 1)], axis=0)
    sums_t = jnp.transpose(sums)[:64, :]
    leaves_t = -sums_t[:32] / (sums_t[32:] + reg_lambda)
    leaves = jnp.transpose(leaves_t)
    for n in range(8):
        leaves_ref[n] = leaves[2 * n : 2 * n + 2, :]
    far_copy.wait_recv()

    def update(i, carry):
        at = pl.ds(pl.multiple_of(i * LANE_BLOCK, LANE_BLOCK), LANE_BLOCK)
        count = far_flag[0, :, at] + far_flag[1, :, at]
        slot = nodes_ref[:, at] * 2 + jnp.where(count > 0.5, 1, 0)
        slot_hot = jnp.where(iota16 == slot, one, zero).astype(jnp.bfloat16)
        new_ref[:, at] = logits_ref[:, at] + step_size * exact_dot(leaves_t, slot_hot, NN)
        return carry

    lax.fori_loop(0, rows // LANE_BLOCK, update, 0)
    stores[0].start()
    stores[1].start()

    lane_in = lax.broadcasted_iota(jnp.int32, (128, 128), 0)
    lane_out = lax.broadcasted_iota(jnp.int32, (128, 128), 1)
    same = (lane_in // BINS) == (lane_out // BINS)
    bin_in, bin_out = lane_in % BINS, lane_out % BINS
    as_weights = lambda mask: jnp.where(mask, one, zero).astype(jnp.bfloat16)
    lower = as_weights(same & (bin_in < bin_out) & (bin_in < BINS - 1))
    every = as_weights(same)
    last = as_weights(same & (bin_in == BINS - 1))
    lane = lax.broadcasted_iota(jnp.int32, (1, 128), 1)
    for pair in range(2):
        owned = hist[4 * pair + 2 * z0 + 1, z1, 2 * y + z2]
        for d in (1, 2, 3):
            slot = direct_buf.at[pair, d]
            remote(slot, slot, direct_send.at[0, 0, 0], direct_recv.at[pair, d], z_peer2).wait_recv()
            owned = owned + direct_buf[pair, d]
        left_base = exact_dot(owned, lower, NN)
        node_total = exact_dot(owned, every, NN)
        left_miss = left_base + exact_dot(owned, last, NN)
        parent = ratio(node_total)
        gain_left = (ratio(left_miss) + ratio(node_total - left_miss) - parent) / 64.0
        gain_right = (ratio(left_base) + ratio(node_total - left_base) - parent) / 64.0
        gain_ref[0, 2 * pair : 2 * pair + 1, :] = jnp.where(
            lane < BINS, gain_left, pltpu.roll(gain_right, BINS, 1)
        )
        gain_ref[0, 2 * pair + 1 : 2 * pair + 2, :] = jnp.where(
            lane < BINS, pltpu.roll(gain_left, BINS, 1), gain_right
        )

    stores[2].start()
    for stage in (flags, along_x, in_group, along_z):
        stage[2]()
    far_copy.wait_send()
    pair_copy.wait_send()
    for k in range(4):
        core_copy(k).wait_send()
    for u in range(8):
        for colour in range(2):
            y1_copy(u, colour, 0).wait_send()
            y1_copy(u, colour, 1).wait_send()
            y2_copy(u, colour).wait_send()
    for u in range(8):

        @pl.when(z0 != chunk_of(u) % 2)
        def _():
            z1_copy(u).wait_send()

    for pair in range(2):
        for nodes in range(2):
            for high in range(2):
                d, copy = direct_copy(pair, nodes, high)

                @pl.when(d != 0)
                def _():
                    copy.wait_send()

    for store in stores:
        store.wait()


def move(new_ref, gain_ref, leaves_ref, new_out, gain_out, leaves_out, new_held, gain_held, leaves_held, sems):
    width = new_ref.shape[1] // 4
    parts = [(leaves_ref, leaves_held, leaves_out), (gain_ref, gain_held, gain_out)]
    for i in range(4):
        at = (slice(None), pl.ds(i * width, width))
        parts.append((new_ref.at[at], new_held.at[at], new_out.at[at]))
    loads = [pltpu.make_async_copy(a, b, sems.at[0, i]) for i, (a, b, _) in enumerate(parts)]
    stores = [pltpu.make_async_copy(b, c, sems.at[1, i]) for i, (_, b, c) in enumerate(parts)]
    for load in loads:
        load.start()
    for load, store in zip(loads, stores):
        load.wait()
        store.start()
    for store in stores:
        store.wait()


def local(logits, labels, node_ids, bin_codes, split_feature, split_bin, split_missing):
    rows = logits.shape[0]
    f32, i32 = jnp.float32, jnp.int32
    hbm = pl.BlockSpec(memory_space=pl.ANY)
    dma = pltpu.SemaphoreType.DMA
    out_shape = (
        jax.ShapeDtypeStruct((32, rows), f32),
        jax.ShapeDtypeStruct((1, 4, 128), f32),
        jax.ShapeDtypeStruct((8, 2, 32), f32),
    )
    results = pl.pallas_call(
        kernel,
        out_shape=out_shape,
        in_specs=[hbm] * 7,
        out_specs=(hbm, hbm, hbm),
        scratch_shapes=[
            pltpu.VMEM((32, rows), f32),
            pltpu.VMEM((1, 4, 128), f32),
            pltpu.VMEM((8, 2, 32), f32),
            pltpu.SMEM((8,), i32),
            pltpu.SMEM((8,), i32),
            pltpu.SMEM((8,), i32),
            pltpu.VMEM((32, rows), f32),
            pltpu.VMEM((1, rows), i32),
            pltpu.VMEM((1, rows), i32),
            pltpu.VMEM((32, rows), i32),
            pltpu.VMEM((512, rows), jnp.bfloat16),
            pltpu.VMEM((256, rows), jnp.bfloat16),
            pltpu.VMEM((8, 2, 8, 64, 128), f32),
            pltpu.VMEM((4, 2, 8, 64, 128), f32),
            pltpu.VMEM((8, 2, 2, 2, 32, 128), f32),
            pltpu.VMEM((8, 2, 2, 32, 128), f32),
            pltpu.VMEM((8, 2, 64, 128), f32),
            pltpu.VMEM((2, 4, 64, 128), f32),
            pltpu.VMEM((4, 1, rows), f32),
            pltpu.VMEM((2, 1, rows), f32),
            pltpu.VMEM((4, 8, 128), f32),
            pltpu.VMEM((16, 8, 128), f32),
            pltpu.VMEM((2, 8, 128), f32),
            pltpu.VMEM((4, 8, 128), f32),
            dma((7,)),
            dma((3,)),
            dma((4,)),
            dma((4,)),
            dma((8, 2, 2)),
            dma((8, 2, 2)),
            dma((8, 2)),
            dma((8, 2)),
            dma((8,)),
            dma((8,)),
            dma((2, 2, 2)),
            dma((2, 4)),
            dma((3,)),
            dma((4,)),
            dma((1,)),
            dma((1,)),
            dma((3,)),
            dma((4,)),
            dma((15,)),
            dma((16,)),
            dma((1,)),
            dma((1,)),
            dma((3,)),
            dma((4,)),
            pltpu.SemaphoreType.REGULAR,
            pltpu.SemaphoreType.REGULAR,
        ],
        compiler_params=pltpu.CompilerParams(
            collective_id=0, has_side_effects=True, vmem_limit_bytes=56 * 1024 * 1024
        ),
    )(
        split_feature,
        split_bin,
        split_missing,
        logits.T,
        labels.reshape(1, rows),
        node_ids.reshape(1, rows),
        bin_codes.T,
    )
    new_t, gains, leaves = pl.pallas_call(
        move,
        out_shape=out_shape,
        in_specs=[hbm] * 3,
        out_specs=(hbm, hbm, hbm),
        scratch_shapes=[
            pltpu.VMEM((32, rows), f32),
            pltpu.VMEM((1, 4, 128), f32),
            pltpu.VMEM((8, 2, 32), f32),
            dma((2, 6)),
        ],
    )(*results)
    return new_t.T, gains, leaves


def solution(mesh):
    return jax.shard_map(
        local,
        mesh=mesh,
        in_specs=(P("rows", None), P("rows"), P("rows"), P("rows", "feat"), P(), P(), P()),
        out_specs=(P("rows", None), P("rows", "feat", None), P()),
        check_vma=False,
    )
```
